32 devices in a mesh: space: 16 (over z, x, core), slab: 2 (over y).
Axes of the slice: x: 2, y: 2, z: 4, core: 2. Of those that a mesh axis runs over, the one named last changes fastest.
Arguments:
- charges: float32 [8192], P(('space', 'slab')), may hold values from -4 to 4
- fractions: float32 [3, 8192], P(None, ('space', 'slab')), may hold values from 0 to 1
- cell_x: int32 [8192], P(('space', 'slab')), may hold values from 0 to 15
- cell_y: int32 [8192], P(('space', 'slab')), may hold values from 0 to 7
- cell_z: int32 [8192], P(('space', 'slab')), may hold values from 0 to 127
- destination: int32 [8192, 1], P(('space', 'slab')), may hold values from 0 to 15; in each aligned block of 256 rows (0 to 255, 256 to 511, ...) at most 32 rows name the same one
Outputs:
- energy: float32 [8192], P(('space', 'slab'))
- forces: float32 [3, 8192], P(None, ('space', 'slab'))
The draws below stay inside these ranges and needn't reach their ends.
Inputs may be any that keep to these rules, and one draw needn't show every extreme that they name: `destination`: among the atoms of one device no block is named by more than 32 atoms, and some block is named by exactly 32 of them.
All inputs are finite; a program needn't handle non-finite values.
Results may differ from the reference program's by a relative error of at most 0.0003.
Values sent between devices are 32-bit elements; how exact they have to be, the bound alone decides.
A program may use at most 128 MiB of HBM per device.

```python
import math
import jax
import jax.numpy as jnp
import numpy as np
from jax import lax

CX = 16
NY = 8
CZ = 128
ATOM_DEV = 256
NX = 256
NZ = 256
ATOMS = 8192
SLOT = 32
N_SPACE = 16
N_SLAB = 2


def set_ends(values, key, least, high):
    place = [jax.random.randint(jax.random.fold_in(key, axis), (), 0, length) for axis, length in enumerate(values.shape)]
    main_axis = values.shape.index(max(values.shape))
    neighbour = place[:main_axis] + [(place[main_axis] + 1) % values.shape[main_axis]] + place[main_axis + 1:]
    return values.at[tuple(place)].set(least).at[tuple(neighbour)].set(high)


def block_scale(own_key, shape, pieces, smallest, high):
    loudness = 1.0
    for dim, blocks in pieces:
        steps = jax.random.uniform(jax.random.fold_in(jax.random.fold_in(own_key, 6), dim), (blocks,), jnp.float32, smallest / len(pieces), high / len(pieces))
        loudness = loudness * jnp.repeat(jnp.exp(steps), shape[dim] // blocks).reshape((-1,) + (1,) * (len(shape) - 1 - dim))
    return loudness


def shared_out(stream_key, own, number, rows, count, top, bound, skew):
    ranking = jax.random.permutation(stream_key, count)
    heavy_load, common = shares(count, rows * top, bound, skew, True), shares(count, rows * top, bound, skew, False)
    places = jnp.arange(count)

    def named(lengths, offset_by):
        used = int((lengths > 0).sum())
        fixed = max(1, used // 4)
        shifted = fixed + (places - fixed + offset_by * (used - fixed)) % max(1, count - fixed)
        return jnp.zeros((count,), jnp.int32).at[ranking[jnp.where(places < fixed, places, shifted)]].set(jnp.asarray(lengths, jnp.int32))

    lengths = jnp.where(number % 4 == 0, named(heavy_load, number // 4), named(common, number - number // 4 - 1))
    mixed = jax.random.permutation(jax.random.fold_in(own, 3), count)
    giver, taker = mixed[0:count // 2 * 2:2], mixed[1:count // 2 * 2:2]
    margin = jnp.minimum(lengths[giver] - 1, bound - lengths[taker]) // 2
    margin = jnp.where((giver == ranking[0]) | (taker == ranking[0]) | (lengths[taker] == 0), 0, jnp.maximum(margin, 0))
    shifted = jax.random.randint(jax.random.fold_in(own, 4), (count // 2,), 0, 1 << 20) % (margin + 1)
    lengths = lengths.at[giver].add(-shifted).at[taker].add(shifted)
    items = jnp.searchsorted(jnp.cumsum(lengths), jnp.arange(rows * top), side="right").astype(jnp.int32)
    listing = items.reshape(top, rows).T
    listing = listing[jax.random.permutation(jax.random.fold_in(own, 1), rows)]
    offset_by = jax.random.randint(jax.random.fold_in(own, 2), (rows, 1), 0, top)
    return jnp.take_along_axis(listing, (jnp.arange(top)[None, :] + offset_by) % top, axis=1)


def shares(count, total, reach, slope, full):
    loads = [(1 << 20) // math.isqrt(rank ** slope) + 1 for rank in range(1, count + 1)]
    largest = reach if full else min(reach, max(-(-total // count), total * loads[0] // sum(loads)))
    least = 1 if total - largest >= count - 1 else 0
    holding, surplus = [largest] + [least] * (count - 1), total - largest - least * (count - 1)
    while surplus > 0:
        movable = [i for i in range(1, count) if holding[i] < largest] or [i for i in range(1, count) if holding[i] < reach]
        mass, budget = sum([loads[i] for i in movable]), surplus
        for i in movable:
            addition = min(reach - holding[i], max(1, budget * loads[i] // mass), surplus)
            holding[i] = holding[i] + addition
            surplus = surplus - addition
    return np.array(holding)


def bell_draw(key, shape, spread, bound, shards=(), kind=jnp.bfloat16):
    array = spread * jax.random.normal(key, shape, jnp.float32)
    if shards:
        array = array * block_scale(key, shape, shards, -0.22, 0.18)
    return jnp.clip(array, -bound, bound).astype(kind)


def setup_inputs(seed: int = 0) -> dict:
    keys = jax.random.split(jax.random.key(seed), 7)
    charges = bell_draw(keys[0], (ATOMS,), 1.0, 4.0, ((0, 32),), jnp.float32)
    fractions = jnp.clip(1.0 * jax.random.uniform(keys[1], (3, ATOMS), jnp.float32) ** block_scale(keys[1], (3, ATOMS), ((1, 32),), -0.2, 0.2), 0.0, 1.0)
    cell_x = set_ends(jax.random.randint(keys[2], (ATOMS,), 0, CX), jax.random.fold_in(keys[2], 1), 0, CX - 1).astype(jnp.int32)
    cell_y = set_ends(jax.random.randint(keys[3], (ATOMS,), 0, NY), jax.random.fold_in(keys[3], 1), 0, NY - 1).astype(jnp.int32)
    cell_z = set_ends(jax.random.randint(keys[4], (ATOMS,), 0, CZ), jax.random.fold_in(keys[4], 1), 0, CZ - 1).astype(jnp.int32)
    destination_keys = jax.random.split(jax.random.fold_in(keys[5], 1), ATOMS // ATOM_DEV)
    destination_turns = jax.random.permutation(jax.random.fold_in(keys[5], 3), ATOMS // ATOM_DEV)
    destination = jax.vmap(lambda own, number: shared_out(jax.random.fold_in(keys[5], 2), own, number, ATOM_DEV, N_SPACE, 1, SLOT, 2))(destination_keys, destination_turns).reshape((ATOMS, 1))
    return dict(charges=charges, fractions=fractions, cell_x=cell_x, cell_y=cell_y, cell_z=cell_z, destination=destination)


coulomb = 332.0636 / 2.5
coarse_weights = (0.125, 0.5, 0.75, 0.5, 0.125)

def smooth_inverse(radius):
    square = radius * radius
    inside_part = 1.875 - 1.25 * square + 0.375 * square * square
    return jnp.where(radius < 1.0, inside_part, 1.0 / jnp.maximum(radius, 1.0))

def stencil_table(level_index, float_type):
    offsets = jnp.arange(9, dtype=jnp.int32) - 4
    squares = offsets * offsets
    summed = squares[:, None, None] + squares[None, :, None] + squares[None, None, :]
    distance = jnp.sqrt(summed.astype(float_type)) * 2.0 ** level_index
    cutoff = 2.0 * 2.0 ** level_index
    return coulomb * (smooth_inverse(distance / cutoff) / cutoff - smooth_inverse(distance / (2.0 * cutoff)) / (2.0 * cutoff))

def spline(offset):
    complement = 1.0 - offset
    offset_cube = offset * offset * offset
    weights = jnp.stack([complement * complement * complement / 6.0, (3.0 * offset_cube - 6.0 * offset * offset + 4.0) / 6.0, (-3.0 * offset_cube + 3.0 * offset * offset + 3.0 * offset + 1.0) / 6.0, offset_cube / 6.0])
    slopes = jnp.stack([-complement * complement / 2.0, (3.0 * offset * offset - 4.0 * offset) / 2.0, (-3.0 * offset * offset + 2.0 * offset + 1.0) / 2.0, offset * offset / 2.0])
    return (weights, slopes)

def pad_dim(grid_in, axis_dim, before, behind):
    widths = [(0, 0)] * grid_in.ndim
    widths[axis_dim] = (before, behind)
    return jnp.pad(grid_in, widths)

def restrict_dim(grid_in, axis_dim, start_at, count_out):
    summed = None
    for offset_index in range(5):
        first_cell = offset_index - 2 - start_at
        slice_part = lax.slice_in_dim(grid_in, first_cell, first_cell + 2 * count_out - 1, 2, axis_dim)
        weighted = coarse_weights[offset_index] * slice_part
        summed = weighted if summed is None else summed + weighted
    return summed

def prolong_dim(grid_in, axis_dim, lead_pad, tail_pad, count_out):
    doubled = list(grid_in.shape)
    doubled[axis_dim] = 2 * doubled[axis_dim]
    upsampled = jnp.stack([grid_in, jnp.zeros_like(grid_in)], axis=axis_dim + 1).reshape(doubled)
    upsampled = pad_dim(upsampled, axis_dim, lead_pad, tail_pad)
    summed = None
    for offset_index in range(5):
        slice_part = lax.slice_in_dim(upsampled, offset_index, offset_index + count_out, 1, axis_dim)
        weighted = coarse_weights[offset_index] * slice_part
        summed = weighted if summed is None else summed + weighted
    return summed

def convolve(grid_in, kernel_table):
    full_shape = tuple((length + 8 for length in grid_in.shape))
    kernel_grid = jnp.zeros(full_shape, grid_in.dtype).at[:9, :9, :9].set(kernel_table.astype(grid_in.dtype))
    kernel_grid = jnp.roll(kernel_grid, (-4, -4, -4), axis=(0, 1, 2))
    padded = jnp.pad(grid_in, ((0, 8), (0, 8), (0, 8)))
    result = jnp.fft.irfftn(jnp.fft.rfftn(padded) * jnp.fft.rfftn(kernel_grid), s=full_shape)
    return result[:grid_in.shape[0], :grid_in.shape[1], :grid_in.shape[2]].astype(grid_in.dtype)

def reference(charges, fractions, cell_x, cell_y, cell_z, destination):
    atom_total = charges.shape[0]
    source = jnp.arange(atom_total, dtype=jnp.int32) // ATOM_DEV
    slab_of = source % N_SLAB
    base_x = destination[:, 0] * CX + cell_x
    base_y = cell_y
    base_z = slab_of * CZ + cell_z
    weight_x, slope_x = spline(fractions[0])
    weight_y, slope_y = spline(fractions[1])
    weight_z, slope_z = spline(fractions[2])
    corner_z = lax.broadcasted_iota(jnp.int32, (4, atom_total), 0) + base_z[None, :]
    spread_grid = jnp.zeros((NX + 3, NY + 3, NZ + 3), charges.dtype)
    for step_x in range(4):
        for step_y in range(4):
            amount = (charges * weight_x[step_x] * weight_y[step_y])[None, :] * weight_z
            spread_grid = spread_grid.at[(base_x + step_x)[None, :], (base_y + step_y)[None, :], corner_z].add(amount)
    charge_grid = spread_grid[1:NX + 1, 1:NY + 1, 1:NZ + 1]
    coarse = jnp.pad(charge_grid, 2)
    coarse = restrict_dim(coarse, 0, -2, NX // 2)
    coarse = restrict_dim(coarse, 1, -2, NY // 2)
    coarse = restrict_dim(coarse, 2, -2, NZ // 2)
    coarse_potential = convolve(coarse, stencil_table(1, charges.dtype))
    lifted = prolong_dim(coarse_potential, 0, 2, 2, NX)
    lifted = prolong_dim(lifted, 1, 2, 2, NY)
    lifted = prolong_dim(lifted, 2, 2, 2, NZ)
    potential = convolve(charge_grid, stencil_table(0, charges.dtype)) + lifted
    field_pad = jnp.pad(potential, ((1, 2), (1, 2), (1, 2)))
    value = jnp.zeros_like(charges)
    grad_x = jnp.zeros_like(charges)
    grad_y = jnp.zeros_like(charges)
    grad_z = jnp.zeros_like(charges)
    for step_x in range(4):
        for step_y in range(4):
            picked = field_pad[(base_x + step_x)[None, :], (base_y + step_y)[None, :], corner_z]
            along_w = lax.optimization_barrier(jnp.sum(weight_z * picked, axis=0))
            along_d = lax.optimization_barrier(jnp.sum(slope_z * picked, axis=0))
            value = value + weight_x[step_x] * weight_y[step_y] * along_w
            grad_x = grad_x + slope_x[step_x] * weight_y[step_y] * along_w
            grad_y = grad_y + weight_x[step_x] * slope_y[step_y] * along_w
            grad_z = grad_z + weight_x[step_x] * weight_y[step_y] * along_d
    energy = 0.5 * charges * value
    forces = jnp.stack([-charges * grad_x, -charges * grad_y, -charges * grad_z])
    return (energy, forces)
```

```python
import functools

import jax
import jax.numpy as jnp
import numpy as np
from jax import lax
from jax.experimental import pallas as pl
from jax.experimental.pallas import tpu as pltpu
from jax.sharding import PartitionSpec as P

CX = 16
NY = 8
CZ = 128
LANES = 128
WIDE = 2 * CZ
COULOMB = 332.0636 / 2.5
B0, B1, B2 = 0.75, 0.5, 0.125
OUT_X = CX + 3
REACH = 12
SIDE = REACH + 2
EXT_X = REACH + CX + REACH + 1
OUT_C = CX // 2 + 3
EXT_C = OUT_C + 8
FINE_S = sorted({a * a + b * b for a in range(5) for b in range(5)})
COARSE_S = sorted({a * a + b * b for a in range(5) for b in range(4)})
FULL_BELOW = 13
FINE_FULL = sum(s < FULL_BELOW for s in FINE_S)
COARSE_FULL = sum(s < FULL_BELOW for s in COARSE_S)
LEAD, TAIL = CZ + 16, 16
MESH = pl.DeviceIdType.MESH
F32 = jnp.float32
BF16 = jnp.bfloat16


def np_gamma(r):
    sq = r * r
    return np.where(r < 1.0, 1.875 - 1.25 * sq + 0.375 * sq * sq, 1.0 / np.maximum(r, 1.0))


def np_stencil(squares, level):
    r = np.sqrt(squares.astype(np.float64)) * 2.0**level
    c = 2.0 * 2.0**level
    return COULOMB * (np_gamma(r / c) / c - np_gamma(r / (2 * c)) / (2 * c))


def np_cells(count):
    lane = np.arange(count)
    return np.where(lane < 3 * count // 4, lane, lane - count)


def tables():
    def banded(cells, level, sums):
        lag = cells[:, None] - cells[None, :]
        parts = [np.where(abs(lag) <= 4, np_stencil(s + lag * lag, level), 0.0) for s in sums]
        return np.stack(parts).astype(np.float32)

    def split(t, full):
        high = t.astype(BF16)
        low = (t - high.astype(np.float32)).astype(BF16)
        return np.concatenate([high, low[:full]], axis=0)

    fine_cells, coarse_cells = np_cells(WIDE), np_cells(LANES)
    off = abs(fine_cells[:, None] - 2 * coarse_cells[None, :])
    rz = np.where(off == 0, B0, np.where(off == 1, B1, np.where(off == 2, B2, 0.0))).astype(BF16)
    fine = split(banded(fine_cells, 0, FINE_S), FINE_FULL)
    fine = np.concatenate([fine[:, :LEAD], fine[:, WIDE - TAIL :]], axis=1)
    return fine, split(banded(coarse_cells, 1, COARSE_S), COARSE_FULL), rz


def two(x):
    high = x.astype(BF16)
    return high, (x - high.astype(F32)).astype(BF16)


PLAIN = (((1,), (0,)), ((), ()))
TURNED = (((1,), (1,)), ((), ()))


def dot1(a, b, dims=PLAIN):
    return lax.dot_general(a, b, dims, preferred_element_type=F32)


def dot3(a, b, dims=PLAIN):
    return dot1(a[0], b[0], dims) + (dot1(a[0], b[1], dims) + dot1(a[1], b[0], dims))


def three_rows(x):
    high = x.astype(BF16).astype(F32)
    rest = x - high
    mid = rest.astype(BF16).astype(F32)
    return jnp.concatenate([high, mid, rest - mid], axis=0).astype(BF16)


def shift_y(x, step):
    if step == 0:
        return x
    rolled = pltpu.roll(x, (-step) % NY, 1)
    y = lax.broadcasted_iota(jnp.int32, x.shape, 1)
    keep = (y < NY - step) if step > 0 else (y >= -step)
    return jnp.where(keep, rolled, 0.0)


def pair_y(x, step):
    if step == 0:
        return x
    return shift_y(x, step) + shift_y(x, -step)


def rows2(x):
    return x.reshape(x.shape[0] * x.shape[1], x.shape[2])


def kernel(
    spaces, slabs, deltas, slot_size,
    charge_hbm, frac_hbm, x_hbm, y_hbm, z_hbm, dest_hbm, fine_hbm, coarse_hbm, rz_hbm,
    out_ref,
    charge_in, frac_in, x_in, y_in, z_in, dest_in, rz_ref, fine_tab, coarse_tab, place, send_buf, stage_buf, relay_buf, recv_buf, own_buf, left_buf, right_buf, res_buf, ret_buf,
    in_sem, tab_sem, self_sem, plane_send, plane_recv, send_sem, recv_sem, halo_send, halo_recv, res_sem, ret_sem,
):
    i = lax.axis_index("space")
    l = lax.axis_index("slab")
    groups = len(deltas)
    atoms = charge_in.shape[1]
    slots = spaces * slot_size
    tiles = slots // LANES
    per_tile = LANES // slot_size

    block = per_tile
    plane_of, in_plane = i // block, lax.rem(i, block)
    width = block * LANES

    def each(first, count=spaces):
        return pl.loop(first, count, unroll=count <= 16)

    def plane_peer(k):
        return (lax.rem(plane_of + k, tiles) * block + in_plane, l)

    def peer(k, g):
        return (plane_of * block + lax.rem(in_plane + k, block), lax.rem(l + deltas[g], slabs))

    barrier = pltpu.get_barrier_semaphore()
    for k in range(1, tiles):
        pl.semaphore_signal(barrier, inc=1, device_id=plane_peer(k), device_id_type=MESH)
    for g in reversed(range(groups)):
        first = 1 if g == 0 else 0

        @each(first, block)
        def _(k):
            pl.semaphore_signal(barrier, inc=1, device_id=peer(k, g), device_id_type=MESH)

    arguments = (
        (charge_hbm, charge_in), (frac_hbm, frac_in), (x_hbm, x_in),
        (y_hbm, y_in), (z_hbm, z_in), (dest_hbm, dest_in),
    )
    arriving = [
        pltpu.make_async_copy(a, b, in_sem.at[n]) for n, (a, b) in enumerate(arguments)
    ]
    for copy in arriving:
        copy.start()
    fine_copy = pltpu.make_async_copy(
        fine_hbm.at[:, pl.ds(0, LEAD)], fine_tab.at[:, pl.ds(0, LEAD)], tab_sem.at[0]
    )
    fine_copy2 = pltpu.make_async_copy(
        fine_hbm.at[:, pl.ds(LEAD, TAIL)], fine_tab.at[:, pl.ds(WIDE - TAIL, TAIL)], tab_sem.at[3]
    )
    coarse_copy = pltpu.make_async_copy(coarse_hbm, coarse_tab, tab_sem.at[1])
    fine_copy.start()
    fine_copy2.start()
    coarse_copy.start()
    rz_copy = pltpu.make_async_copy(rz_hbm, rz_ref, tab_sem.at[2])
    rz_copy.start()

    @pl.when(i == 0)
    def _():
        left_buf[...] = jnp.zeros_like(left_buf)

    @pl.when(i == spaces - 1)
    def _():
        right_buf[...] = jnp.zeros_like(right_buf)

    for copy in arriving:
        copy.wait()
    dest = dest_in[...].astype(F32)
    payload = jnp.concatenate(
        [
            charge_in[...],
            frac_in[...],
            x_in[...].astype(F32),
            y_in[...].astype(F32),
            z_in[...].astype(F32),
            dest,
        ],
        axis=0,
    )
    chosen = (
        lax.broadcasted_iota(jnp.int32, (spaces, atoms), 0).astype(F32) == dest
    ).astype(F32)
    earlier = (
        lax.broadcasted_iota(jnp.int32, (atoms, atoms), 0)
        < lax.broadcasted_iota(jnp.int32, (atoms, atoms), 1)
    ).astype(F32).astype(BF16)
    counts = dot1(chosen.astype(BF16), earlier)
    rank = jnp.sum(chosen * counts, axis=0, keepdims=True)
    slot = dest * float(slot_size) + rank
    place[...] = (
        lax.broadcasted_iota(jnp.int32, (slots, atoms), 0).astype(F32) == slot
    ).astype(F32).astype(BF16)
    parts = dot1(three_rows(payload), place[...], TURNED)
    packed = parts[0:8] + parts[8:16] + parts[16:24]
    lane_part = lax.broadcasted_iota(jnp.int32, (8, LANES), 1) // slot_size
    row_part = lax.rem(lax.broadcasted_iota(jnp.int32, (8, LANES), 0), per_tile)
    columns = min(8, per_tile)

    def compact(value, count, out):
        for q in range(block):
            tile = value[:, q * LANES : (q + 1) * LANES]
            turned = [pltpu.roll(tile, n * slot_size, 1) if n else tile for n in range(per_tile)]
            for r in range(tiles):
                merged = jnp.zeros((8, LANES), F32)
                for c in range(columns):
                    here = (lane_part == c) & (row_part == c)
                    merged = jnp.where(here, turned[(c - r) % per_tile], merged)
                for n in range(-(-count // per_tile)):
                    rows = merged[n * columns : (n + 1) * columns]
                    out[r * block + q, n : n + 1] = jnp.sum(rows, axis=0, keepdims=True)

    for q in range(tiles):
        send_buf[q] = packed[:, q * LANES : (q + 1) * LANES]

    fine_tab[:, LEAD : WIDE - TAIL] = jnp.zeros(
        (fine_tab.shape[0], WIDE - TAIL - LEAD, WIDE), BF16
    )
    pl.semaphore_wait(barrier, tiles - 1 + groups * block - 1)

    def plane_copy(k, source):
        target = plane_peer(k)
        return pltpu.make_async_remote_copy(
            src_ref=send_buf.at[lax.rem(plane_of + k, tiles)],
            dst_ref=stage_buf.at[source],
            send_sem=plane_send.at[k],
            recv_sem=plane_recv.at[source],
            device_id=target,
            device_id_type=MESH,
        )

    for k in range(1, tiles):
        plane_copy(k, plane_of).start()
    stage_buf[plane_of] = send_buf[plane_of]
    for k in range(1, tiles):
        plane_copy(k, lax.rem(plane_of - k + tiles, tiles)).wait_recv()
    staged = [stage_buf[q] for q in range(tiles)]
    for n in range(block):
        merged = jnp.zeros((8, LANES), F32)
        for q in range(tiles):
            turn = (q - n) * slot_size % LANES
            turned = pltpu.roll(staged[q], turn, 1) if turn else staged[q]
            merged = jnp.where(lane_part == q, turned, merged)
        relay_buf[n] = merged

    def atom_copy(k, g, source):
        return pltpu.make_async_remote_copy(
            src_ref=relay_buf.at[lax.rem(in_plane + k, block)],
            dst_ref=recv_buf.at[g, source],
            send_sem=send_sem.at[g, k],
            recv_sem=recv_sem.at[g, source],
            device_id=peer(k, g),
            device_id_type=MESH,
        )

    for g in reversed(range(groups)):

        @each(1 if g == 0 else 0, block)
        def _(k):
            atom_copy(k, g, in_plane).start()

    recv_buf[0, in_plane] = relay_buf[in_plane]

    def regroup(piece_of):
        out = []
        for q in range(tiles):
            total = jnp.zeros((8, LANES), F32)
            for r in range(per_tile):
                piece = piece_of(q * per_tile + r)
                repeated = [
                    jnp.broadcast_to(piece[n : n + 1], (columns, LANES))
                    for n in range(piece.shape[0])
                ]
                while len(repeated) * columns < 8:
                    repeated.append(jnp.zeros((columns, LANES), F32))
                spread = jnp.concatenate(repeated, axis=0)
                for c in range(columns):
                    turn = (r - c) % per_tile * slot_size
                    turned = pltpu.roll(spread, turn, 1) if turn else spread
                    total = jnp.where((lane_part == r) & (row_part == c), turned, total)
            out.append(total)
        return jnp.concatenate(out, axis=1)

    def spline(t):
        u = 1.0 - t
        t2 = t * t
        t3 = t2 * t
        w = (
            u * u * u / 6.0,
            (3.0 * t3 - 6.0 * t2 + 4.0) / 6.0,
            (-3.0 * t3 + 3.0 * t2 + 3.0 * t + 1.0) / 6.0,
            t3 / 6.0,
        )
        s = (
            -u * u / 2.0,
            (3.0 * t2 - 4.0 * t) / 2.0,
            (-3.0 * t2 + 2.0 * t + 1.0) / 2.0,
            t2 / 2.0,
        )
        return w, s

    def spread_rows(weights, row, position):
        total = jnp.zeros(position.shape, F32)
        for k in range(4):
            total = jnp.where(position == float(k), weights[k][row : row + 1], total)
        return total

    row_x = lax.broadcasted_iota(jnp.int32, (24, width), 0).astype(F32)
    row_y = lax.broadcasted_iota(jnp.int32, (NY, width), 0).astype(F32) + 1.0

    own_rows = ((0, CZ + 16), (WIDE - 16, WIDE))
    side_rows = ((0, 16), (CZ - 16, CZ + 16), (WIDE - 16, WIDE))

    def z_matrix(weights, base, pieces):
        halves = ([], [])
        done = 0
        for first, end in pieces:
            if first > done:
                for h in halves:
                    h.append(jnp.zeros((first - done, width), BF16))
            row = lax.broadcasted_iota(jnp.int32, (end - first, width), 0) + first
            row = (row if end <= 3 * WIDE // 4 else row - WIDE).astype(F32) + 1.0
            for h, part in zip(halves, two(spread_rows(weights, 3, row - base))):
                h.append(part)
            done = end
        return tuple(jnp.concatenate(h, axis=0) for h in halves)

    for g in range(groups):

        @each(1 if g == 0 else 0, block)
        def _(k):
            atom_copy(k, g, lax.rem(in_plane - k + block, block)).wait_recv()


    planes, zs = [], []
    for g in range(groups):
        got = jnp.concatenate([recv_buf[g, n] for n in range(block)], axis=1)
        w, s = spline(got)
        mx = spread_rows(w, 1, row_x - got[4:5])
        my = spread_rows(w, 2, row_y - got[5:6])
        z_off = ((lax.rem(l - deltas[g] + slabs, slabs) - l) * CZ).astype(F32)
        z_base = got[6:7] + z_off
        mz = z_matrix(w, z_base, side_rows if g else own_rows)
        if g == 0:
            charge = got[0:1]
            own = (w, s, got, mx, my)
        cx = got[0:1] * mx
        plane = jnp.concatenate([cx[x : x + 1] * my for x in range(OUT_X)], axis=0)
        planes.append(two(plane))
        zs.append(mz)
    mz_split = zs[0]
    plane2 = [jnp.concatenate([p[h] for p in planes], axis=1) for h in range(2)]
    z2 = [jnp.concatenate([z[h] for z in zs], axis=1) for h in range(2)]
    own_buf[...] = dot3(plane2, z2, TURNED).reshape(OUT_X, NY, WIDE)

    right_copy = pltpu.make_async_remote_copy(
        src_ref=own_buf.at[pl.ds(OUT_X - SIDE, SIDE)], dst_ref=left_buf,
        send_sem=halo_send.at[0], recv_sem=halo_recv.at[0],
        device_id=(lax.rem(i + 1, spaces), l), device_id_type=MESH,
    )
    left_copy = pltpu.make_async_remote_copy(
        src_ref=own_buf.at[pl.ds(0, SIDE)], dst_ref=right_buf,
        send_sem=halo_send.at[1], recv_sem=halo_recv.at[1],
        device_id=(lax.rem(i + spaces - 1, spaces), l), device_id_type=MESH,
    )

    @pl.when(i < spaces - 1)
    def _():
        right_copy.start()

    @pl.when(i > 0)
    def _():
        left_copy.start()

    w, s, got, mx, my = own
    dx = spread_rows(s, 1, row_x - got[4:5])
    dy = spread_rows(s, 2, row_y - got[5:6])
    dz_split = z_matrix(s, got[6:7], own_rows)
    fine_copy.wait()
    fine_copy2.wait()
    coarse_copy.wait()
    rz_copy.wait()

    @pl.when(i > 0)
    def _():
        right_copy.wait_recv()

    @pl.when(i < spaces - 1)
    def _():
        left_copy.wait_recv()

    def inside(shape, first_x, block_x, block_z):
        ax = lax.broadcasted_iota(jnp.int32, shape, 0) + (i * block_x + first_x)
        az = lax.broadcasted_iota(jnp.int32, shape, 2)
        lanes = shape[2]
        az = jnp.where(az < 3 * lanes // 4, az, az - lanes) + l * block_z
        return (ax >= 0) & (ax < spaces * block_x) & (az >= 0) & (az < slabs * block_z)

    mid = own_buf[...]
    left = left_buf[...]
    right = right_buf[...]
    over = SIDE - REACH + 1
    grid = jnp.concatenate(
        [
            left[: SIDE - over],
            left[SIDE - over :] + mid[:over],
            mid[over : OUT_X - over],
            mid[OUT_X - over :] + right[:over],
            right[over:],
        ],
        axis=0,
    )
    grid = jnp.where(inside(grid.shape, -REACH, CX, CZ), grid, 0.0)

    def stencil(parts, table, kinds, full):
        depth = table.shape[1]
        high = table[:kinds].reshape(kinds * depth, table.shape[2])
        low = table[kinds:].reshape(full * depth, table.shape[2])
        a, b = parts
        near = full * depth
        return dot1(a, high) + (dot1(a[:, :near], low) + dot1(b, high[:near]))

    coarse = []
    for n in range(EXT_C):
        at = 2 * n + 2
        coarse.append(
            B0 * grid[at : at + 1]
            + B1 * (grid[at - 1 : at] + grid[at + 1 : at + 2])
            + B2 * (grid[at - 2 : at - 1] + grid[at + 2 : at + 3])
        )
    coarse = jnp.concatenate(coarse, axis=0)
    coarse = B0 * coarse + B1 * pair_y(coarse, 1) + B2 * pair_y(coarse, 2)
    high, low = two(rows2(coarse))
    rz = rz_ref[...]
    coarse = (dot1(high, rz) + dot1(low, rz)).reshape(EXT_C, NY, LANES)
    coarse = jnp.where(inside(coarse.shape, -5, CX // 2, CZ // 2), coarse, 0.0)

    def stack(source, out_count, step_y, reach_y, sums):
        shifted = [pair_y(source, step_y * d) if step_y * d < NY else None for d in range(reach_y)]
        highs, lows = [], []
        for square in sums:
            total = None
            for d in range(5):
                for e in range(reach_y):
                    if d * d + e * e != square:
                        continue
                    v = shifted[e]
                    term = v[4 + d : 4 + d + out_count]
                    if d:
                        term = term + v[4 - d : 4 - d + out_count]
                    total = term if total is None else total + term
            total = rows2(total)
            if square < FULL_BELOW:
                a, b = two(total)
                lows.append(b)
            else:
                a = total.astype(BF16)
            highs.append(a)
        return jnp.concatenate(highs, axis=1), jnp.concatenate(lows, axis=1)

    lifted = stencil(
        stack(coarse, OUT_C, 2, 4, COARSE_S), coarse_tab, len(COARSE_S), COARSE_FULL
    ).reshape(OUT_C, NY, LANES)
    even = lax.rem(lax.broadcasted_iota(jnp.int32, lifted.shape, 1), 2) == 0
    lifted = jnp.where(inside(lifted.shape, -1, CX // 2, CZ // 2) & even, lifted, 0.0)
    lifted = B0 * lifted + B1 * pair_y(lifted, 1) + B2 * pair_y(lifted, 2)
    high, low = two(rows2(lifted))
    lifted = (dot1(high, rz, TURNED) + dot1(low, rz, TURNED)).reshape(OUT_C, NY, WIDE)
    fine_lift = []
    for m in range(-1, CX + 2):
        n = m // 2 + 1
        if m % 2:
            fine_lift.append(B1 * (lifted[n : n + 1] + lifted[n + 1 : n + 2]))
        else:
            fine_lift.append(
                B0 * lifted[n : n + 1] + B2 * (lifted[n - 1 : n] + lifted[n + 1 : n + 2])
            )
    around = grid[REACH - 5 : REACH - 5 + OUT_X + 8]
    potential = stencil(
        stack(around, OUT_X, 1, 5, FINE_S), fine_tab, len(FINE_S), FINE_FULL
    ).reshape(OUT_X, NY, WIDE)
    potential = potential + jnp.concatenate(fine_lift, axis=0)
    potential = jnp.where(inside(potential.shape, -1, CX, CZ), potential, 0.0)

    pot = two(rows2(potential))
    through_w = dot3(pot, mz_split)
    through_d = dot3(pot, dz_split)
    along_w = along_dx = along_dz = jnp.zeros((NY, width), F32)
    for x in range(OUT_X):
        tw = through_w[x * NY : (x + 1) * NY]
        td = through_d[x * NY : (x + 1) * NY]
        along_w = along_w + mx[x : x + 1] * tw
        along_dx = along_dx + dx[x : x + 1] * tw
        along_dz = along_dz + mx[x : x + 1] * td

    def down(v):
        return jnp.sum(v, axis=0, keepdims=True)

    results = jnp.concatenate(
        [
            0.5 * charge * down(my * along_w),
            -charge * down(my * along_dx),
            -charge * down(dy * along_w),
            -charge * down(my * along_dz),
            jnp.zeros((4, width), F32),
        ],
        axis=0,
    )
    compact(results, 4, res_buf)

    def result_copy(k, source):
        target = lax.rem(i + k, spaces)
        return pltpu.make_async_remote_copy(
            src_ref=res_buf.at[target], dst_ref=ret_buf.at[source],
            send_sem=res_sem.at[k], recv_sem=ret_sem.at[source],
            device_id=(target, l), device_id_type=MESH,
        )

    @each(1)
    def _(k):
        result_copy(k, i).start()

    own_results = pltpu.make_async_copy(res_buf.at[i], ret_buf.at[i], self_sem.at[0])
    own_results.start()

    for g in range(groups):

        @each(1 if g == 0 else 0, block)
        def _(k):
            atom_copy(k, g, in_plane).wait_send()

    for k in range(1, tiles):
        plane_copy(k, plane_of).wait_send()

    @pl.when(i < spaces - 1)
    def _():
        right_copy.wait_send()

    @pl.when(i > 0)
    def _():
        left_copy.wait_send()

    @each(1)
    def _(k):
        result_copy(k, lax.rem(i - k + spaces, spaces)).wait_recv()

    own_results.wait()
    back = regroup(lambda j: ret_buf[j])
    parts = dot1(three_rows(back), place[...])
    final = parts[0:8] + parts[8:16] + parts[16:24]
    out_ref[...] = final

    @each(1)
    def _(k):
        result_copy(k, i).wait_send()


def per_device(spaces, slabs, charges, fractions, cell_x, cell_y, cell_z, destination):
    atoms = charges.shape[0]
    slot_size = 2 * atoms // spaces
    slots = spaces * slot_size
    deltas = (0,) if slabs == 1 else (0, 1) if slabs == 2 else (0, 1, slabs - 1)
    groups = len(deltas)
    fine, coarse, rz = tables()
    vmem = pl.BlockSpec(memory_space=pltpu.VMEM)
    result_rows = -(-4 * slot_size // LANES)
    tiles, block = slots // LANES, LANES // slot_size
    hbm = pl.BlockSpec(memory_space=pl.ANY)
    out = pl.pallas_call(
        functools.partial(kernel, spaces, slabs, deltas, slot_size),
        out_shape=pltpu.VMEM((8, atoms), F32),
        in_specs=[hbm] * 9,
        out_specs=vmem,
        scratch_shapes=[
            pltpu.VMEM((1, atoms), F32),
            pltpu.VMEM((3, atoms), F32),
            pltpu.VMEM((1, atoms), jnp.int32),
            pltpu.VMEM((1, atoms), jnp.int32),
            pltpu.VMEM((1, atoms), jnp.int32),
            pltpu.VMEM((1, atoms), jnp.int32),
            pltpu.VMEM(rz.shape, BF16),
            pltpu.VMEM((fine.shape[0], WIDE, WIDE), BF16),
            pltpu.VMEM(coarse.shape, BF16),
            pltpu.VMEM((slots, atoms), BF16),
            pltpu.VMEM((tiles, 8, LANES), F32),
            pltpu.VMEM((tiles, 8, LANES), F32),
            pltpu.VMEM((block, 8, LANES), F32),
            pltpu.VMEM((groups, block, 8, LANES), F32),
            pltpu.VMEM((OUT_X, NY, WIDE), F32),
            pltpu.VMEM((SIDE, NY, WIDE), F32),
            pltpu.VMEM((SIDE, NY, WIDE), F32),
            pltpu.VMEM((spaces, result_rows, LANES), F32),
            pltpu.VMEM((spaces, result_rows, LANES), F32),
            pltpu.SemaphoreType.DMA((6,)),
            pltpu.SemaphoreType.DMA((4,)),
            pltpu.SemaphoreType.DMA((1,)),
            pltpu.SemaphoreType.DMA((tiles,)),
            pltpu.SemaphoreType.DMA((tiles,)),
            pltpu.SemaphoreType.DMA((groups, block)),
            pltpu.SemaphoreType.DMA((groups, block)),
            pltpu.SemaphoreType.DMA((2,)),
            pltpu.SemaphoreType.DMA((2,)),
            pltpu.SemaphoreType.DMA((spaces,)),
            pltpu.SemaphoreType.DMA((spaces,)),
        ],
        compiler_params=pltpu.CompilerParams(collective_id=0, has_side_effects=True),
        name="multilevel",
    )(
        charges.reshape(1, atoms),
        fractions,
        cell_x.reshape(1, atoms),
        cell_y.reshape(1, atoms),
        cell_z.reshape(1, atoms),
        destination.reshape(1, atoms),
        jnp.asarray(fine),
        jnp.asarray(coarse),
        jnp.asarray(rz),
    )
    return out[0], out[1:4]


def solution(mesh):
    both = ("space", "slab")
    return jax.shard_map(
        functools.partial(per_device, mesh.shape["space"], mesh.shape["slab"]),
        mesh=mesh,
        in_specs=(P(both), P(None, both), P(both), P(both), P(both), P(both, None)),
        out_specs=(P(both), P(None, both)),
        check_vma=False,
    )
```

```python
import functools

import jax
import jax.numpy as jnp
import numpy as np
from jax import lax
from jax.experimental import pallas as pl
from jax.experimental.pallas import tpu as pltpu
from jax.sharding import PartitionSpec as P

CX = 16
NY = 8
CZ = 128
LANES = 128
WIDE = 2 * CZ
COULOMB = 332.0636 / 2.5
B0, B1, B2 = 0.75, 0.5, 0.125
OUT_X = CX + 3
REACH = 12
SIDE = REACH + 2
EXT_X = REACH + CX + REACH + 1
OUT_C = CX // 2 + 3
EXT_C = OUT_C + 8
FINE_S = sorted({a * a + b * b for a in range(5) for b in range(5)})
COARSE_S = sorted({a * a + b * b for a in range(5) for b in range(4)})
FULL_BELOW = 13
FINE_FULL = sum(s < FULL_BELOW for s in FINE_S)
COARSE_FULL = sum(s < FULL_BELOW for s in COARSE_S)
LEAD, TAIL = CZ + 16, 16
MESH = pl.DeviceIdType.MESH
F32 = jnp.float32
BF16 = jnp.bfloat16


def np_gamma(r):
    sq = r * r
    return np.where(r < 1.0, 1.875 - 1.25 * sq + 0.375 * sq * sq, 1.0 / np.maximum(r, 1.0))


def np_stencil(squares, level):
    r = np.sqrt(squares.astype(np.float64)) * 2.0**level
    c = 2.0 * 2.0**level
    return COULOMB * (np_gamma(r / c) / c - np_gamma(r / (2 * c)) / (2 * c))


def np_cells(count):
    lane = np.arange(count)
    return np.where(lane < 3 * count // 4, lane, lane - count)


def tables():
    def banded(cells, level, sums):
        lag = cells[:, None] - cells[None, :]
        parts = [np.where(abs(lag) <= 4, np_stencil(s + lag * lag, level), 0.0) for s in sums]
        return np.stack(parts).astype(np.float32)

    def split(t, full):
        high = t.astype(BF16)
        low = (t - high.astype(np.float32)).astype(BF16)
        return np.concatenate([high, low[:full]], axis=0)

    fine_cells, coarse_cells = np_cells(WIDE), np_cells(LANES)
    off = abs(fine_cells[:, None] - 2 * coarse_cells[None, :])
    rz = np.where(off == 0, B0, np.where(off == 1, B1, np.where(off == 2, B2, 0.0))).astype(BF16)
    fine = split(banded(fine_cells, 0, FINE_S), FINE_FULL)
    fine = np.concatenate([fine[:, :LEAD], fine[:, WIDE - TAIL :]], axis=1)
    return fine, split(banded(coarse_cells, 1, COARSE_S), COARSE_FULL), rz


def two(x):
    high = x.astype(BF16)
    return high, (x - high.astype(F32)).astype(BF16)


PLAIN = (((1,), (0,)), ((), ()))
TURNED = (((1,), (1,)), ((), ()))


def dot1(a, b, dims=PLAIN):
    return lax.dot_general(a, b, dims, preferred_element_type=F32)


def dot3(a, b, dims=PLAIN):
    return dot1(a[0], b[0], dims) + (dot1(a[0], b[1], dims) + dot1(a[1], b[0], dims))


def three_rows(x):
    high = x.astype(BF16).astype(F32)
    rest = x - high
    mid = rest.astype(BF16).astype(F32)
    return jnp.concatenate([high, mid, rest - mid], axis=0).astype(BF16)


def shift_y(x, step):
    if step == 0:
        return x
    rolled = pltpu.roll(x, (-step) % NY, 1)
    y = lax.broadcasted_iota(jnp.int32, x.shape, 1)
    keep = (y < NY - step) if step > 0 else (y >= -step)
    return jnp.where(keep, rolled, 0.0)


def pair_y(x, step):
    if step == 0:
        return x
    return shift_y(x, step) + shift_y(x, -step)


def rows2(x):
    return x.reshape(x.shape[0] * x.shape[1], x.shape[2])


def kernel(
    spaces, slabs, deltas, slot_size,
    charge_hbm, frac_hbm, x_hbm, y_hbm, z_hbm, dest_hbm, fine_hbm, coarse_hbm, rz_hbm,
    out_ref,
    charge_in, frac_in, x_in, y_in, z_in, dest_in, rz_ref, fine_tab, coarse_tab, place, send_buf, recv_buf, res_buf, ret_buf,
    in_sem, tab_sem, self_sem, send_sem, recv_sem, res_sem, ret_sem,
):
    i = lax.axis_index("space")
    l = lax.axis_index("slab")
    groups = len(deltas)
    atoms = charge_in.shape[1]
    slots = spaces * slot_size
    tiles = slots // LANES
    per_tile = LANES // slot_size

    def each(first):
        return pl.loop(first, spaces, unroll=spaces <= 16)

    def peer(k, g):
        return (lax.rem(i + k, spaces), lax.rem(l + deltas[g], slabs))

    barrier = pltpu.get_barrier_semaphore()
    for g in reversed(range(groups)):
        first = 1 if g == 0 else 0

        @each(first)
        def _(k):
            pl.semaphore_signal(barrier, inc=1, device_id=peer(k, g), device_id_type=MESH)

    arguments = (
        (charge_hbm, charge_in), (frac_hbm, frac_in), (x_hbm, x_in),
        (y_hbm, y_in), (z_hbm, z_in), (dest_hbm, dest_in),
    )
    arriving = [
        pltpu.make_async_copy(a, b, in_sem.at[n]) for n, (a, b) in enumerate(arguments)
    ]
    for copy in arriving:
        copy.start()
    fine_copy = pltpu.make_async_copy(
        fine_hbm.at[:, pl.ds(0, LEAD)], fine_tab.at[:, pl.ds(0, LEAD)], tab_sem.at[0]
    )
    fine_copy2 = pltpu.make_async_copy(
        fine_hbm.at[:, pl.ds(LEAD, TAIL)], fine_tab.at[:, pl.ds(WIDE - TAIL, TAIL)], tab_sem.at[3]
    )
    coarse_copy = pltpu.make_async_copy(coarse_hbm, coarse_tab, tab_sem.at[1])
    fine_copy.start()
    fine_copy2.start()
    coarse_copy.start()
    rz_copy = pltpu.make_async_copy(rz_hbm, rz_ref, tab_sem.at[2])
    rz_copy.start()

    for edge in (0, spaces + 1):
        send_buf[edge] = jnp.zeros(send_buf.shape[1:], F32)

    for copy in arriving:
        copy.wait()
    dest = dest_in[...].astype(F32)
    payload = jnp.concatenate(
        [
            charge_in[...],
            frac_in[...],
            x_in[...].astype(F32),
            y_in[...].astype(F32),
            z_in[...].astype(F32),
            dest,
        ],
        axis=0,
    )
    chosen = (
        lax.broadcasted_iota(jnp.int32, (spaces, atoms), 0).astype(F32) == dest
    ).astype(F32)
    earlier = (
        lax.broadcasted_iota(jnp.int32, (atoms, atoms), 0)
        < lax.broadcasted_iota(jnp.int32, (atoms, atoms), 1)
    ).astype(F32).astype(BF16)
    counts = dot1(chosen.astype(BF16), earlier)
    rank = jnp.sum(chosen * counts, axis=0, keepdims=True)
    slot = dest * float(slot_size) + rank
    place[...] = (
        lax.broadcasted_iota(jnp.int32, (slots, atoms), 0).astype(F32) == slot
    ).astype(F32).astype(BF16)
    parts = dot1(three_rows(payload), place[...], TURNED)
    packed = parts[0:8] + parts[8:16] + parts[16:24]
    lane_part = lax.broadcasted_iota(jnp.int32, (8, LANES), 1) // slot_size
    row_part = lax.rem(lax.broadcasted_iota(jnp.int32, (8, LANES), 0), per_tile)
    columns = min(8, per_tile)

    def compact(value, count, out, skip=0):
        for q in range(tiles):
            tile = value[:, q * LANES : (q + 1) * LANES]
            turned = [pltpu.roll(tile, n * slot_size, 1) if n else tile for n in range(per_tile)]
            for r in range(per_tile):
                merged = jnp.zeros((8, LANES), F32)
                for c in range(columns):
                    here = (lane_part == c) & (row_part == c)
                    merged = jnp.where(here, turned[(c - r) % per_tile], merged)
                for n in range(-(-count // per_tile)):
                    rows = merged[n * columns : (n + 1) * columns]
                    out[q * per_tile + r + skip, n : n + 1] = jnp.sum(rows, axis=0, keepdims=True)

    compact(packed, 8, send_buf, 1)

    fine_tab[:, LEAD : WIDE - TAIL] = jnp.zeros(
        (fine_tab.shape[0], WIDE - TAIL - LEAD, WIDE), BF16
    )
    pl.semaphore_wait(barrier, groups * spaces - 1)

    def atom_copy(k, g):
        target = peer(k, g)
        return pltpu.make_async_remote_copy(
            src_ref=send_buf.at[pl.ds(target[0], 3)],
            dst_ref=recv_buf.at[g, i],
            send_sem=send_sem.at[g, k],
            recv_sem=recv_sem.at[g, i],
            device_id=target,
            device_id_type=MESH,
        )

    def atom_wait(k, g):
        source = lax.rem(i - k + spaces, spaces)
        return pltpu.make_async_remote_copy(
            src_ref=send_buf.at[pl.ds(0, 3)],
            dst_ref=recv_buf.at[g, source],
            send_sem=send_sem.at[g, k],
            recv_sem=recv_sem.at[g, source],
            device_id=peer(k, g),
            device_id_type=MESH,
        )

    for g in reversed(range(groups)):

        @each(1 if g == 0 else 0)
        def _(k):
            atom_copy(k, g).start()

    own_atoms = pltpu.make_async_copy(send_buf.at[pl.ds(i, 3)], recv_buf.at[0, i], self_sem.at[0])
    own_atoms.start()

    def regroup(piece_of):
        out = []
        for q in range(tiles):
            total = jnp.zeros((8, LANES), F32)
            for r in range(per_tile):
                piece = piece_of(q * per_tile + r)
                repeated = [
                    jnp.broadcast_to(piece[n : n + 1], (columns, LANES))
                    for n in range(piece.shape[0])
                ]
                while len(repeated) * columns < 8:
                    repeated.append(jnp.zeros((columns, LANES), F32))
                spread = jnp.concatenate(repeated, axis=0)
                for c in range(columns):
                    turn = (r - c) % per_tile * slot_size
                    turned = pltpu.roll(spread, turn, 1) if turn else spread
                    total = jnp.where((lane_part == r) & (row_part == c), turned, total)
            out.append(total)
        return jnp.concatenate(out, axis=1)

    def spline(t):
        u = 1.0 - t
        t2 = t * t
        t3 = t2 * t
        w = (
            u * u * u / 6.0,
            (3.0 * t3 - 6.0 * t2 + 4.0) / 6.0,
            (-3.0 * t3 + 3.0 * t2 + 3.0 * t + 1.0) / 6.0,
            t3 / 6.0,
        )
        s = (
            -u * u / 2.0,
            (3.0 * t2 - 4.0 * t) / 2.0,
            (-3.0 * t2 + 2.0 * t + 1.0) / 2.0,
            t2 / 2.0,
        )
        return w, s

    def spread_rows(weights, row, position):
        total = jnp.zeros(position.shape, F32)
        for k in range(4):
            total = jnp.where(position == float(k), weights[k][row : row + 1], total)
        return total

    row_x = lax.broadcasted_iota(jnp.int32, (24, slots), 0).astype(F32)
    row_y = lax.broadcasted_iota(jnp.int32, (NY, slots), 0).astype(F32) + 1.0

    own_rows = ((0, CZ + 16), (WIDE - 16, WIDE))
    side_rows = ((0, 16), (CZ - 16, CZ + 16), (WIDE - 16, WIDE))

    def z_matrix(weights, base, pieces):
        halves = ([], [])
        done = 0
        for first, end in pieces:
            if first > done:
                for h in halves:
                    h.append(jnp.zeros((first - done, slots), BF16))
            row = lax.broadcasted_iota(jnp.int32, (end - first, slots), 0) + first
            row = (row if end <= 3 * WIDE // 4 else row - WIDE).astype(F32) + 1.0
            for h, part in zip(halves, two(spread_rows(weights, 3, row - base))):
                h.append(part)
            done = end
        return tuple(jnp.concatenate(h, axis=0) for h in halves)

    for g in range(groups):

        @each(1 if g == 0 else 0)
        def _(k):
            atom_wait(k, g).wait_recv()

    own_atoms.wait()

    def spread(part, first_row, rows):
        planes, zs, kept = [], [], None
        for g in range(groups):
            got = regroup(lambda j: recv_buf[g, j, part])
            w, s = spline(got)
            mx = spread_rows(w, 1, row_x - got[4:5])
            my = spread_rows(w, 2, row_y - got[5:6])
            z_off = ((lax.rem(l - deltas[g] + slabs, slabs) - l) * CZ).astype(F32)
            z_base = got[6:7] + z_off
            mz = z_matrix(w, z_base, side_rows if g else own_rows)
            if g == 0:
                kept = (w, s, got, mx, my, mz)
            cx = got[0:1] * mx
            plane = jnp.concatenate(
                [cx[x : x + 1] * my for x in range(first_row, first_row + rows)], axis=0
            )
            planes.append(two(plane))
            zs.append(mz)
        plane2 = [jnp.concatenate([p[h] for p in planes], axis=1) for h in range(2)]
        z2 = [jnp.concatenate([z[h] for z in zs], axis=1) for h in range(2)]
        return dot3(plane2, z2, TURNED).reshape(rows, NY, WIDE), kept

    mid, own = spread(1, 0, OUT_X)
    left, _ = spread(0, OUT_X - SIDE, SIDE)
    right, _ = spread(2, 0, SIDE)

    w, s, got, mx, my, mz_split = own
    charge = got[0:1]
    dx = spread_rows(s, 1, row_x - got[4:5])
    dy = spread_rows(s, 2, row_y - got[5:6])
    dz_split = z_matrix(s, got[6:7], own_rows)
    fine_copy.wait()
    fine_copy2.wait()
    coarse_copy.wait()
    rz_copy.wait()

    def inside(shape, first_x, block_x, block_z):
        ax = lax.broadcasted_iota(jnp.int32, shape, 0) + (i * block_x + first_x)
        az = lax.broadcasted_iota(jnp.int32, shape, 2)
        lanes = shape[2]
        az = jnp.where(az < 3 * lanes // 4, az, az - lanes) + l * block_z
        return (ax >= 0) & (ax < spaces * block_x) & (az >= 0) & (az < slabs * block_z)

    over = SIDE - REACH + 1
    grid = jnp.concatenate(
        [
            left[: SIDE - over],
            left[SIDE - over :] + mid[:over],
            mid[over : OUT_X - over],
            mid[OUT_X - over :] + right[:over],
            right[over:],
        ],
        axis=0,
    )
    grid = jnp.where(inside(grid.shape, -REACH, CX, CZ), grid, 0.0)

    def stencil(parts, table, kinds, full):
        depth = table.shape[1]
        high = table[:kinds].reshape(kinds * depth, table.shape[2])
        low = table[kinds:].reshape(full * depth, table.shape[2])
        a, b = parts
        near = full * depth
        return dot1(a, high) + (dot1(a[:, :near], low) + dot1(b, high[:near]))

    coarse = []
    for n in range(EXT_C):
        at = 2 * n + 2
        coarse.append(
            B0 * grid[at : at + 1]
            + B1 * (grid[at - 1 : at] + grid[at + 1 : at + 2])
            + B2 * (grid[at - 2 : at - 1] + grid[at + 2 : at + 3])
        )
    coarse = jnp.concatenate(coarse, axis=0)
    coarse = B0 * coarse + B1 * pair_y(coarse, 1) + B2 * pair_y(coarse, 2)
    high, low = two(rows2(coarse))
    rz = rz_ref[...]
    coarse = (dot1(high, rz) + dot1(low, rz)).reshape(EXT_C, NY, LANES)
    coarse = jnp.where(inside(coarse.shape, -5, CX // 2, CZ // 2), coarse, 0.0)

    def stack(source, out_count, step_y, reach_y, sums):
        shifted = [pair_y(source, step_y * d) if step_y * d < NY else None for d in range(reach_y)]
        highs, lows = [], []
        for square in sums:
            total = None
            for d in range(5):
                for e in range(reach_y):
                    if d * d + e * e != square:
                        continue
                    v = shifted[e]
                    term = v[4 + d : 4 + d + out_count]
                    if d:
                        term = term + v[4 - d : 4 - d + out_count]
                    total = term if total is None else total + term
            total = rows2(total)
            if square < FULL_BELOW:
                a, b = two(total)
                lows.append(b)
            else:
                a = total.astype(BF16)
            highs.append(a)
        return jnp.concatenate(highs, axis=1), jnp.concatenate(lows, axis=1)

    lifted = stencil(
        stack(coarse, OUT_C, 2, 4, COARSE_S), coarse_tab, len(COARSE_S), COARSE_FULL
    ).reshape(OUT_C, NY, LANES)
    even = lax.rem(lax.broadcasted_iota(jnp.int32, lifted.shape, 1), 2) == 0
    lifted = jnp.where(inside(lifted.shape, -1, CX // 2, CZ // 2) & even, lifted, 0.0)
    lifted = B0 * lifted + B1 * pair_y(lifted, 1) + B2 * pair_y(lifted, 2)
    high, low = two(rows2(lifted))
    lifted = (dot1(high, rz, TURNED) + dot1(low, rz, TURNED)).reshape(OUT_C, NY, WIDE)
    fine_lift = []
    for m in range(-1, CX + 2):
        n = m // 2 + 1
        if m % 2:
            fine_lift.append(B1 * (lifted[n : n + 1] + lifted[n + 1 : n + 2]))
        else:
            fine_lift.append(
                B0 * lifted[n : n + 1] + B2 * (lifted[n - 1 : n] + lifted[n + 1 : n + 2])
            )
    around = grid[REACH - 5 : REACH - 5 + OUT_X + 8]
    potential = stencil(
        stack(around, OUT_X, 1, 5, FINE_S), fine_tab, len(FINE_S), FINE_FULL
    ).reshape(OUT_X, NY, WIDE)
    potential = potential + jnp.concatenate(fine_lift, axis=0)
    potential = jnp.where(inside(potential.shape, -1, CX, CZ), potential, 0.0)

    pot = two(rows2(potential))
    through_w = dot3(pot, mz_split)
    through_d = dot3(pot, dz_split)
    along_w = along_dx = along_dz = jnp.zeros((NY, slots), F32)
    for x in range(OUT_X):
        tw = through_w[x * NY : (x + 1) * NY]
        td = through_d[x * NY : (x + 1) * NY]
        along_w = along_w + mx[x : x + 1] * tw
        along_dx = along_dx + dx[x : x + 1] * tw
        along_dz = along_dz + mx[x : x + 1] * td

    def down(v):
        return jnp.sum(v, axis=0, keepdims=True)

    results = jnp.concatenate(
        [
            0.5 * charge * down(my * along_w),
            -charge * down(my * along_dx),
            -charge * down(dy * along_w),
            -charge * down(my * along_dz),
            jnp.zeros((4, slots), F32),
        ],
        axis=0,
    )
    compact(results, 4, res_buf)

    def result_copy(k, source):
        target = lax.rem(i + k, spaces)
        return pltpu.make_async_remote_copy(
            src_ref=res_buf.at[target], dst_ref=ret_buf.at[source],
            send_sem=res_sem.at[k], recv_sem=ret_sem.at[source],
            device_id=(target, l), device_id_type=MESH,
        )

    @each(1)
    def _(k):
        result_copy(k, i).start()

    own_results = pltpu.make_async_copy(res_buf.at[i], ret_buf.at[i], self_sem.at[1])
    own_results.start()

    for g in range(groups):

        @each(1 if g == 0 else 0)
        def _(k):
            atom_wait(k, g).wait_send()

    @each(1)
    def _(k):
        result_copy(k, lax.rem(i - k + spaces, spaces)).wait_recv()

    own_results.wait()
    back = regroup(lambda j: ret_buf[j])
    parts = dot1(three_rows(back), place[...])
    final = parts[0:8] + parts[8:16] + parts[16:24]
    out_ref[...] = final

    @each(1)
    def _(k):
        result_copy(k, i).wait_send()


def per_device(spaces, slabs, charges, fractions, cell_x, cell_y, cell_z, destination):
    atoms = charges.shape[0]
    slot_size = 2 * atoms // spaces
    slots = spaces * slot_size
    deltas = (0,) if slabs == 1 else (0, 1) if slabs == 2 else (0, 1, slabs - 1)
    groups = len(deltas)
    fine, coarse, rz = tables()
    vmem = pl.BlockSpec(memory_space=pltpu.VMEM)
    atom_rows, result_rows = (-(-n * slot_size // LANES) for n in (8, 4))
    hbm = pl.BlockSpec(memory_space=pl.ANY)
    out = pl.pallas_call(
        functools.partial(kernel, spaces, slabs, deltas, slot_size),
        out_shape=pltpu.VMEM((8, atoms), F32),
        in_specs=[hbm] * 9,
        out_specs=vmem,
        scratch_shapes=[
            pltpu.VMEM((1, atoms), F32),
            pltpu.VMEM((3, atoms), F32),
            pltpu.VMEM((1, atoms), jnp.int32),
            pltpu.VMEM((1, atoms), jnp.int32),
            pltpu.VMEM((1, atoms), jnp.int32),
            pltpu.VMEM((1, atoms), jnp.int32),
            pltpu.VMEM(rz.shape, BF16),
            pltpu.VMEM((fine.shape[0], WIDE, WIDE), BF16),
            pltpu.VMEM(coarse.shape, BF16),
            pltpu.VMEM((slots, atoms), BF16),
            pltpu.VMEM((spaces + 2, atom_rows, LANES), F32),
            pltpu.VMEM((groups, spaces, 3, atom_rows, LANES), F32),
            pltpu.VMEM((spaces, result_rows, LANES), F32),
            pltpu.VMEM((spaces, result_rows, LANES), F32),
            pltpu.SemaphoreType.DMA((6,)),
            pltpu.SemaphoreType.DMA((4,)),
            pltpu.SemaphoreType.DMA((2,)),
            pltpu.SemaphoreType.DMA((groups, spaces)),
            pltpu.SemaphoreType.DMA((groups, spaces)),
            pltpu.SemaphoreType.DMA((spaces,)),
            pltpu.SemaphoreType.DMA((spaces,)),
        ],
        compiler_params=pltpu.CompilerParams(collective_id=0, has_side_effects=True),
        name="multilevel",
    )(
        charges.reshape(1, atoms),
        fractions,
        cell_x.reshape(1, atoms),
        cell_y.reshape(1, atoms),
        cell_z.reshape(1, atoms),
        destination.reshape(1, atoms),
        jnp.asarray(fine),
        jnp.asarray(coarse),
        jnp.asarray(rz),
    )
    return out[0], out[1:4]


def solution(mesh):
    both = ("space", "slab")
    return jax.shard_map(
        functools.partial(per_device, mesh.shape["space"], mesh.shape["slab"]),
        mesh=mesh,
        in_specs=(P(both), P(None, both), P(both), P(both), P(both), P(both, None)),
        out_specs=(P(both), P(None, both)),
        check_vma=False,
    )
```

```python
import functools

import jax
import jax.numpy as jnp
import numpy as np
from jax import lax
from jax.experimental import pallas as pl
from jax.experimental.pallas import tpu as pltpu
from jax.sharding import PartitionSpec as P

CX = 16
NY = 8
CZ = 128
LANES = 128
WIDE = 2 * CZ
COULOMB = 332.0636 / 2.5
B0, B1, B2 = 0.75, 0.5, 0.125
OUT_X = CX + 3
REACH = 12
SIDE = REACH + 2
EXT_X = REACH + CX + REACH + 1
OUT_C = CX // 2 + 3
EXT_C = OUT_C + 8
FINE_S = sorted({a * a + b * b for a in range(5) for b in range(5)})
COARSE_S = sorted({a * a + b * b for a in range(5) for b in range(4)})
FULL_BELOW = 13
FINE_FULL = sum(s < FULL_BELOW for s in FINE_S)
COARSE_FULL = sum(s < FULL_BELOW for s in COARSE_S)
LEAD, TAIL = CZ + 16, 16
MESH = pl.DeviceIdType.MESH
F32 = jnp.float32
BF16 = jnp.bfloat16


def np_gamma(r):
    sq = r * r
    return np.where(r < 1.0, 1.875 - 1.25 * sq + 0.375 * sq * sq, 1.0 / np.maximum(r, 1.0))


def np_stencil(squares, level):
    r = np.sqrt(squares.astype(np.float64)) * 2.0**level
    c = 2.0 * 2.0**level
    return COULOMB * (np_gamma(r / c) / c - np_gamma(r / (2 * c)) / (2 * c))


def np_cells(count):
    lane = np.arange(count)
    return np.where(lane < 3 * count // 4, lane, lane - count)


def tables():
    def banded(cells, level, sums):
        lag = cells[:, None] - cells[None, :]
        parts = [np.where(abs(lag) <= 4, np_stencil(s + lag * lag, level), 0.0) for s in sums]
        return np.stack(parts).astype(np.float32)

    def split(t, full):
        high = t.astype(BF16)
        low = (t - high.astype(np.float32)).astype(BF16)
        return np.concatenate([high[:full], -high[full:], -low[:full]], axis=0)

    fine_cells, coarse_cells = np_cells(WIDE), np_cells(LANES)
    off = abs(fine_cells[:, None] - 2 * coarse_cells[None, :])
    rz = np.where(off == 0, B0, np.where(off == 1, B1, np.where(off == 2, B2, 0.0))).astype(BF16)
    fine = split(banded(fine_cells, 0, FINE_S), FINE_FULL)
    fine = np.concatenate([fine[:, :LEAD], fine[:, WIDE - TAIL :]], axis=1)
    return fine, split(banded(coarse_cells, 1, COARSE_S), COARSE_FULL), rz


def two(x):
    high = x.astype(BF16)
    return high, (x - high.astype(F32)).astype(BF16)


PLAIN = (((1,), (0,)), ((), ()))
TURNED = (((1,), (1,)), ((), ()))


def dot1(a, b, dims=PLAIN):
    return lax.dot_general(a, b, dims, preferred_element_type=F32)


def two_rows(x):
    high = x.astype(BF16).astype(F32)
    return jnp.concatenate([high, x - high], axis=0).astype(BF16)


def dot3(rows, both, b, dims=PLAIN):
    wide = dot1(both, b[0], dims)
    return wide[:rows] + wide[rows:] - dot1(both[:rows], b[1], dims)


def three_rows(x):
    high = x.astype(BF16).astype(F32)
    rest = x - high
    mid = rest.astype(BF16).astype(F32)
    return jnp.concatenate([high, mid, rest - mid], axis=0).astype(BF16)


def shift_y(x, step):
    if step == 0:
        return x
    rolled = pltpu.roll(x, (-step) % NY, 1)
    y = lax.broadcasted_iota(jnp.int32, x.shape, 1)
    keep = (y < NY - step) if step > 0 else (y >= -step)
    return jnp.where(keep, rolled, 0.0)


def pair_y(x, step):
    if step == 0:
        return x
    return shift_y(x, step) + shift_y(x, -step)


def rows2(x):
    return x.reshape(x.shape[0] * x.shape[1], x.shape[2])


def kernel(
    spaces, slabs, deltas, slot_size,
    charge_hbm, frac_hbm, x_hbm, y_hbm, z_hbm, dest_hbm, fine_hbm, coarse_hbm, rz_hbm,
    out_ref,
    charge_in, frac_in, x_in, y_in, z_in, dest_in, rz_ref, fine_tab, coarse_tab, place, send_buf, recv_buf, res_buf, ret_buf,
    in_sem, tab_sem, self_sem, send_sem, recv_sem, res_sem, ret_sem,
):
    i = lax.axis_index("space")
    l = lax.axis_index("slab")
    groups = len(deltas)
    atoms = charge_in.shape[1]
    slots = spaces * slot_size
    tiles = slots // LANES
    per_tile = LANES // slot_size

    def each(first):
        return pl.loop(first, spaces, unroll=spaces <= 16)

    def peer(k, g):
        return (lax.rem(i + k, spaces), lax.rem(l + deltas[g], slabs))

    barrier = pltpu.get_barrier_semaphore()
    for g in reversed(range(groups)):
        first = 1 if g == 0 else 0

        @each(first)
        def _(k):
            pl.semaphore_signal(barrier, inc=1, device_id=peer(k, g), device_id_type=MESH)

    arguments = (
        (charge_hbm, charge_in), (frac_hbm, frac_in), (x_hbm, x_in),
        (y_hbm, y_in), (z_hbm, z_in), (dest_hbm, dest_in),
    )
    arriving = [
        pltpu.make_async_copy(a, b, in_sem.at[n]) for n, (a, b) in enumerate(arguments)
    ]
    for copy in arriving:
        copy.start()
    fine_copy = pltpu.make_async_copy(
        fine_hbm.at[:, pl.ds(0, LEAD)], fine_tab.at[:, pl.ds(0, LEAD)], tab_sem.at[0]
    )
    fine_copy2 = pltpu.make_async_copy(
        fine_hbm.at[:, pl.ds(LEAD, TAIL)], fine_tab.at[:, pl.ds(WIDE - TAIL, TAIL)], tab_sem.at[3]
    )
    coarse_copy = pltpu.make_async_copy(coarse_hbm, coarse_tab, tab_sem.at[1])
    fine_copy.start()
    fine_copy2.start()
    coarse_copy.start()
    rz_copy = pltpu.make_async_copy(rz_hbm, rz_ref, tab_sem.at[2])
    rz_copy.start()

    for edge in (0, spaces + 1):
        send_buf[edge] = jnp.zeros(send_buf.shape[1:], F32)

    for copy in arriving:
        copy.wait()
    dest = dest_in[...].astype(F32)
    payload = jnp.concatenate(
        [
            charge_in[...],
            frac_in[...],
            x_in[...].astype(F32),
            y_in[...].astype(F32),
            z_in[...].astype(F32),
            dest,
        ],
        axis=0,
    )
    chosen = (
        lax.broadcasted_iota(jnp.int32, (spaces, atoms), 0).astype(F32) == dest
    ).astype(F32)
    earlier = (
        lax.broadcasted_iota(jnp.int32, (atoms, atoms), 0)
        < lax.broadcasted_iota(jnp.int32, (atoms, atoms), 1)
    ).astype(F32).astype(BF16)
    counts = dot1(chosen.astype(BF16), earlier)
    rank = jnp.sum(chosen * counts, axis=0, keepdims=True)
    slot = dest * float(slot_size) + rank
    place[...] = (
        lax.broadcasted_iota(jnp.int32, (slots, atoms), 0).astype(F32) == slot
    ).astype(F32).astype(BF16)
    parts = dot1(three_rows(payload), place[...], TURNED)
    packed = parts[0:8] + parts[8:16] + parts[16:24]
    lane_part = lax.broadcasted_iota(jnp.int32, (8, LANES), 1) // slot_size
    row_part = lax.rem(lax.broadcasted_iota(jnp.int32, (8, LANES), 0), per_tile)
    columns = min(8, per_tile)

    def compact(value, count, out, skip=0):
        for q in range(tiles):
            tile = value[:, q * LANES : (q + 1) * LANES]
            turned = [pltpu.roll(tile, n * slot_size, 1) if n else tile for n in range(per_tile)]
            for r in range(per_tile):
                merged = jnp.zeros((8, LANES), F32)
                for c in range(columns):
                    here = (lane_part == c) & (row_part == c)
                    merged = jnp.where(here, turned[(c - r) % per_tile], merged)
                for n in range(-(-count // per_tile)):
                    rows = merged[n * columns : (n + 1) * columns]
                    out[q * per_tile + r + skip, n : n + 1] = jnp.sum(rows, axis=0, keepdims=True)

    compact(packed, 8, send_buf, 1)

    fine_tab[:, LEAD : WIDE - TAIL] = jnp.zeros(
        (fine_tab.shape[0], WIDE - TAIL - LEAD, WIDE), BF16
    )
    pl.semaphore_wait(barrier, groups * spaces - 1)

    def atom_copy(k, g):
        target = peer(k, g)
        return pltpu.make_async_remote_copy(
            src_ref=send_buf.at[pl.ds(target[0], 3)],
            dst_ref=recv_buf.at[g, i],
            send_sem=send_sem.at[g, k],
            recv_sem=recv_sem.at[g, i],
            device_id=target,
            device_id_type=MESH,
        )

    def atom_wait(k, g):
        source = lax.rem(i - k + spaces, spaces)
        return pltpu.make_async_remote_copy(
            src_ref=send_buf.at[pl.ds(0, 3)],
            dst_ref=recv_buf.at[g, source],
            send_sem=send_sem.at[g, k],
            recv_sem=recv_sem.at[g, source],
            device_id=peer(k, g),
            device_id_type=MESH,
        )

    for g in reversed(range(groups)):

        @each(1 if g == 0 else 0)
        def _(k):
            atom_copy(k, g).start()

    own_atoms = pltpu.make_async_copy(send_buf.at[pl.ds(i, 3)], recv_buf.at[0, i], self_sem.at[0])
    own_atoms.start()

    def regroup(piece_of):
        out = []
        for q in range(tiles):
            total = jnp.zeros((8, LANES), F32)
            for r in range(per_tile):
                piece = piece_of(q * per_tile + r)
                repeated = [
                    jnp.broadcast_to(piece[n : n + 1], (columns, LANES))
                    for n in range(piece.shape[0])
                ]
                while len(repeated) * columns < 8:
                    repeated.append(jnp.zeros((columns, LANES), F32))
                spread = jnp.concatenate(repeated, axis=0)
                for c in range(columns):
                    turn = (r - c) % per_tile * slot_size
                    turned = pltpu.roll(spread, turn, 1) if turn else spread
                    total = jnp.where((lane_part == r) & (row_part == c), turned, total)
            out.append(total)
        return jnp.concatenate(out, axis=1)

    def spline(t):
        u = 1.0 - t
        t2 = t * t
        t3 = t2 * t
        w = (
            u * u * u / 6.0,
            (3.0 * t3 - 6.0 * t2 + 4.0) / 6.0,
            (-3.0 * t3 + 3.0 * t2 + 3.0 * t + 1.0) / 6.0,
            t3 / 6.0,
        )
        s = (
            -u * u / 2.0,
            (3.0 * t2 - 4.0 * t) / 2.0,
            (-3.0 * t2 + 2.0 * t + 1.0) / 2.0,
            t2 / 2.0,
        )
        return w, s

    def spread_rows(weights, row, position):
        total = jnp.zeros(position.shape, F32)
        for k in range(4):
            total = jnp.where(position == float(k), weights[k][row : row + 1], total)
        return total

    row_x = lax.broadcasted_iota(jnp.int32, (24, slots), 0).astype(F32)
    row_y = lax.broadcasted_iota(jnp.int32, (NY, slots), 0).astype(F32) + 1.0

    own_rows = ((0, CZ + 16), (WIDE - 16, WIDE))
    side_rows = ((0, 16), (CZ - 16, CZ + 16), (WIDE - 16, WIDE))

    def z_matrix(weights, base, pieces):
        def packed_rows(v):
            return jnp.broadcast_to(v, (16, slots)).astype(BF16)

        base = packed_rows(base - 1.0)
        highs = [weights[k][3:4].astype(BF16).astype(F32) for k in range(4)]
        lows = [packed_rows(highs[k] - weights[k][3:4]) for k in range(4)]
        highs = [packed_rows(v) for v in highs]
        low_row = lax.broadcasted_iota(jnp.int32, (16, slots), 0).astype(F32)
        halves = ([], [])
        done = 0
        for first, end in pieces:
            if first > done:
                for h in halves:
                    h.append(jnp.zeros((first - done, slots), BF16))
            shift = 0 if end <= 3 * WIDE // 4 else WIDE
            for row in range(first - shift, end - shift, 16):
                lag = (low_row + float(row)).astype(BF16) - base
                high = low = jnp.zeros((16, slots), BF16)
                for k in range(4):
                    here = lag == jnp.array(k, BF16)
                    high = jnp.where(here, highs[k], high)
                    low = jnp.where(here, lows[k], low)
                halves[0].append(high)
                halves[1].append(low)
            done = end
        return tuple(jnp.concatenate(h, axis=0) for h in halves)

    for g in range(groups):

        @each(1 if g == 0 else 0)
        def _(k):
            atom_wait(k, g).wait_recv()

    own_atoms.wait()

    def spread(part, first_row, rows):
        planes, zs, kept = [], [], None
        for g in range(groups):
            got = regroup(lambda j: recv_buf[g, j, part])
            w, s = spline(got)
            mx = spread_rows(w, 1, row_x - got[4:5])
            my = spread_rows(w, 2, row_y - got[5:6])
            z_off = ((lax.rem(l - deltas[g] + slabs, slabs) - l) * CZ).astype(F32)
            z_base = got[6:7] + z_off
            mz = z_matrix(w, z_base, side_rows if g else own_rows)
            if g == 0:
                kept = (w, s, got, mx, my, mz)
            cx = got[0:1] * mx
            plane = jnp.concatenate(
                [cx[x : x + 1] * my for x in range(first_row, first_row + rows)], axis=0
            )
            planes.append(two_rows(plane))
            zs.append(mz)
        plane2 = jnp.concatenate(planes, axis=1)
        z2 = [jnp.concatenate([z[h] for z in zs], axis=1) for h in range(2)]
        return dot3(rows * NY, plane2, z2, TURNED).reshape(rows, NY, WIDE), kept

    mid, own = spread(1, 0, OUT_X)
    left, _ = spread(0, OUT_X - SIDE, SIDE)
    right, _ = spread(2, 0, SIDE)

    w, s, got, mx, my, mz_split = own
    charge = got[0:1]
    dx = spread_rows(s, 1, row_x - got[4:5])
    dy = spread_rows(s, 2, row_y - got[5:6])
    dz_split = z_matrix(s, got[6:7], own_rows)
    fine_copy.wait()
    fine_copy2.wait()
    coarse_copy.wait()
    rz_copy.wait()

    def inside(shape, first_x, block_x, block_z):
        ax = lax.broadcasted_iota(jnp.int32, shape, 0) + (i * block_x + first_x)
        az = lax.broadcasted_iota(jnp.int32, shape, 2)
        lanes = shape[2]
        az = jnp.where(az < 3 * lanes // 4, az, az - lanes) + l * block_z
        return (ax >= 0) & (ax < spaces * block_x) & (az >= 0) & (az < slabs * block_z)

    over = SIDE - REACH + 1
    grid = jnp.concatenate(
        [
            left[: SIDE - over],
            left[SIDE - over :] + mid[:over],
            mid[over : OUT_X - over],
            mid[OUT_X - over :] + right[:over],
            right[over:],
        ],
        axis=0,
    )
    grid = jnp.where(inside(grid.shape, -REACH, CX, CZ), grid, 0.0)

    def stencil(parts, table, full):
        near, far = parts
        rows, depth = far.shape[0], table.shape[1]
        wide = dot1(near, table[:full].reshape(full * depth, table.shape[2]))
        rest = dot1(
            jnp.concatenate([far, near[:rows]], axis=1),
            table[full:].reshape(-1, table.shape[2]),
        )
        return wide[:rows] + wide[rows:] - rest

    coarse = []
    for n in range(EXT_C):
        at = 2 * n + 2
        coarse.append(
            B0 * grid[at : at + 1]
            + B1 * (grid[at - 1 : at] + grid[at + 1 : at + 2])
            + B2 * (grid[at - 2 : at - 1] + grid[at + 2 : at + 3])
        )
    coarse = jnp.concatenate(coarse, axis=0)
    coarse = B0 * coarse + B1 * pair_y(coarse, 1) + B2 * pair_y(coarse, 2)
    high, low = two(rows2(coarse))
    rz = rz_ref[...]
    coarse = (dot1(high, rz) + dot1(low, rz)).reshape(EXT_C, NY, LANES)
    coarse = jnp.where(inside(coarse.shape, -5, CX // 2, CZ // 2), coarse, 0.0)

    def stack(source, out_count, step_y, reach_y, sums):
        shifted = [pair_y(source, step_y * d) if step_y * d < NY else None for d in range(reach_y)]
        near, far = [], []
        for square in sums:
            total = None
            for d in range(5):
                for e in range(reach_y):
                    if d * d + e * e != square:
                        continue
                    v = shifted[e]
                    term = v[4 + d : 4 + d + out_count]
                    if d:
                        term = term + v[4 - d : 4 - d + out_count]
                    total = term if total is None else total + term
            total = rows2(total)
            if square < FULL_BELOW:
                near.append(two_rows(total))
            else:
                far.append(total.astype(BF16))
        return jnp.concatenate(near, axis=1), jnp.concatenate(far, axis=1)

    lifted = stencil(
        stack(coarse, OUT_C, 2, 4, COARSE_S), coarse_tab, COARSE_FULL
    ).reshape(OUT_C, NY, LANES)
    even = lax.rem(lax.broadcasted_iota(jnp.int32, lifted.shape, 1), 2) == 0
    lifted = jnp.where(inside(lifted.shape, -1, CX // 2, CZ // 2) & even, lifted, 0.0)
    lifted = B0 * lifted + B1 * pair_y(lifted, 1) + B2 * pair_y(lifted, 2)
    high, low = two(rows2(lifted))
    lifted = (dot1(high, rz, TURNED) + dot1(low, rz, TURNED)).reshape(OUT_C, NY, WIDE)
    fine_lift = []
    for m in range(-1, CX + 2):
        n = m // 2 + 1
        if m % 2:
            fine_lift.append(B1 * (lifted[n : n + 1] + lifted[n + 1 : n + 2]))
        else:
            fine_lift.append(
                B0 * lifted[n : n + 1] + B2 * (lifted[n - 1 : n] + lifted[n + 1 : n + 2])
            )
    around = grid[REACH - 5 : REACH - 5 + OUT_X + 8]
    potential = stencil(
        stack(around, OUT_X, 1, 5, FINE_S), fine_tab, FINE_FULL
    ).reshape(OUT_X, NY, WIDE)
    potential = potential + jnp.concatenate(fine_lift, axis=0)
    potential = jnp.where(inside(potential.shape, -1, CX, CZ), potential, 0.0)

    pot = two_rows(rows2(potential))
    through_w = dot3(OUT_X * NY, pot, mz_split)
    through_d = dot3(OUT_X * NY, pot, dz_split)
    along_w = along_dx = along_dz = jnp.zeros((NY, slots), F32)
    for x in range(OUT_X):
        tw = through_w[x * NY : (x + 1) * NY]
        td = through_d[x * NY : (x + 1) * NY]
        along_w = along_w + mx[x : x + 1] * tw
        along_dx = along_dx + dx[x : x + 1] * tw
        along_dz = along_dz + mx[x : x + 1] * td

    def down(v):
        return jnp.sum(v, axis=0, keepdims=True)

    results = jnp.concatenate(
        [
            0.5 * charge * down(my * along_w),
            -charge * down(my * along_dx),
            -charge * down(dy * along_w),
            -charge * down(my * along_dz),
            jnp.zeros((4, slots), F32),
        ],
        axis=0,
    )
    compact(results, 4, res_buf)

    def result_copy(k, source):
        target = lax.rem(i + k, spaces)
        return pltpu.make_async_remote_copy(
            src_ref=res_buf.at[target], dst_ref=ret_buf.at[source],
            send_sem=res_sem.at[k], recv_sem=ret_sem.at[source],
            device_id=(target, l), device_id_type=MESH,
        )

    @each(1)
    def _(k):
        result_copy(k, i).start()

    own_results = pltpu.make_async_copy(res_buf.at[i], ret_buf.at[i], self_sem.at[1])
    own_results.start()

    for g in range(groups):

        @each(1 if g == 0 else 0)
        def _(k):
            atom_wait(k, g).wait_send()

    @each(1)
    def _(k):
        result_copy(k, lax.rem(i - k + spaces, spaces)).wait_recv()

    own_results.wait()
    back = regroup(lambda j: ret_buf[j])
    parts = dot1(three_rows(back), place[...])
    final = parts[0:8] + parts[8:16] + parts[16:24]
    out_ref[...] = final

    @each(1)
    def _(k):
        result_copy(k, i).wait_send()


def per_device(spaces, slabs, charges, fractions, cell_x, cell_y, cell_z, destination):
    atoms = charges.shape[0]
    slot_size = 2 * atoms // spaces
    slots = spaces * slot_size
    deltas = (0,) if slabs == 1 else (0, 1) if slabs == 2 else (0, 1, slabs - 1)
    groups = len(deltas)
    fine, coarse, rz = tables()
    vmem = pl.BlockSpec(memory_space=pltpu.VMEM)
    atom_rows, result_rows = (-(-n * slot_size // LANES) for n in (8, 4))
    hbm = pl.BlockSpec(memory_space=pl.ANY)
    out = pl.pallas_call(
        functools.partial(kernel, spaces, slabs, deltas, slot_size),
        out_shape=pltpu.VMEM((8, atoms), F32),
        in_specs=[hbm] * 9,
        out_specs=vmem,
        scratch_shapes=[
            pltpu.VMEM((1, atoms), F32),
            pltpu.VMEM((3, atoms), F32),
            pltpu.VMEM((1, atoms), jnp.int32),
            pltpu.VMEM((1, atoms), jnp.int32),
            pltpu.VMEM((1, atoms), jnp.int32),
            pltpu.VMEM((1, atoms), jnp.int32),
            pltpu.VMEM(rz.shape, BF16),
            pltpu.VMEM((fine.shape[0], WIDE, WIDE), BF16),
            pltpu.VMEM(coarse.shape, BF16),
            pltpu.VMEM((slots, atoms), BF16),
            pltpu.VMEM((spaces + 2, atom_rows, LANES), F32),
            pltpu.VMEM((groups, spaces, 3, atom_rows, LANES), F32),
            pltpu.VMEM((spaces, result_rows, LANES), F32),
            pltpu.VMEM((spaces, result_rows, LANES), F32),
            pltpu.SemaphoreType.DMA((6,)),
            pltpu.SemaphoreType.DMA((4,)),
            pltpu.SemaphoreType.DMA((2,)),
            pltpu.SemaphoreType.DMA((groups, spaces)),
            pltpu.SemaphoreType.DMA((groups, spaces)),
            pltpu.SemaphoreType.DMA((spaces,)),
            pltpu.SemaphoreType.DMA((spaces,)),
        ],
        compiler_params=pltpu.CompilerParams(collective_id=0, has_side_effects=True),
        name="multilevel",
    )(
        charges.reshape(1, atoms),
        fractions,
        cell_x.reshape(1, atoms),
        cell_y.reshape(1, atoms),
        cell_z.reshape(1, atoms),
        destination.reshape(1, atoms),
        jnp.asarray(fine),
        jnp.asarray(coarse),
        jnp.asarray(rz),
    )
    return out[0], out[1:4]


def solution(mesh):
    both = ("space", "slab")
    return jax.shard_map(
        functools.partial(per_device, mesh.shape["space"], mesh.shape["slab"]),
        mesh=mesh,
        in_specs=(P(both), P(None, both), P(both), P(both), P(both), P(both, None)),
        out_specs=(P(both), P(None, both)),
        check_vma=False,
    )
```

```python
import functools

import jax
import jax.numpy as jnp
import numpy as np
from jax import lax
from jax.experimental import pallas as pl
from jax.experimental.pallas import tpu as pltpu
from jax.sharding import PartitionSpec as P

CX = 16
NY = 8
CZ = 128
LANES = 128
WIDE = 2 * CZ
COULOMB = 332.0636 / 2.5
B0, B1, B2 = 0.75, 0.5, 0.125
OUT_X = CX + 3
REACH = 12
SIDE = REACH + 2
EXT_X = REACH + CX + REACH + 1
OUT_C = CX // 2 + 3
EXT_C = OUT_C + 8
FINE_S = sorted({a * a + b * b for a in range(5) for b in range(5)})
COARSE_S = sorted({a * a + b * b for a in range(5) for b in range(4)})
FULL_BELOW = 13
FINE_FULL = sum(s < FULL_BELOW for s in FINE_S)
COARSE_FULL = sum(s < FULL_BELOW for s in COARSE_S)
LEAD, TAIL = CZ + 16, 16
MESH = pl.DeviceIdType.MESH
F32 = jnp.float32
BF16 = jnp.bfloat16


def np_gamma(r):
    sq = r * r
    return np.where(r < 1.0, 1.875 - 1.25 * sq + 0.375 * sq * sq, 1.0 / np.maximum(r, 1.0))


def np_stencil(squares, level):
    r = np.sqrt(squares.astype(np.float64)) * 2.0**level
    c = 2.0 * 2.0**level
    return COULOMB * (np_gamma(r / c) / c - np_gamma(r / (2 * c)) / (2 * c))


def np_cells(count):
    lane = np.arange(count)
    return np.where(lane < 3 * count // 4, lane, lane - count)


def tables():
    def banded(cells, level, sums):
        lag = cells[:, None] - cells[None, :]
        parts = [np.where(abs(lag) <= 4, np_stencil(s + lag * lag, level), 0.0) for s in sums]
        return np.stack(parts).astype(np.float32)

    def split(t, full):
        high = t.astype(BF16)
        low = (t - high.astype(np.float32)).astype(BF16)
        return np.concatenate([high[:full], -high[full:], -low[:full]], axis=0)

    fine_cells, coarse_cells = np_cells(WIDE), np_cells(LANES)
    off = abs(fine_cells[:, None] - 2 * coarse_cells[None, :])
    rz = np.where(off == 0, B0, np.where(off == 1, B1, np.where(off == 2, B2, 0.0))).astype(BF16)
    fine = split(banded(fine_cells, 0, FINE_S), FINE_FULL)
    fine = np.concatenate([fine[:, :LEAD], fine[:, WIDE - TAIL :]], axis=1)
    return fine, split(banded(coarse_cells, 1, COARSE_S), COARSE_FULL), rz


def two(x):
    high = x.astype(BF16)
    return high, (x - high.astype(F32)).astype(BF16)


PLAIN = (((1,), (0,)), ((), ()))
TURNED = (((1,), (1,)), ((), ()))


def dot1(a, b, dims=PLAIN):
    return lax.dot_general(a, b, dims, preferred_element_type=F32)


def two_rows(x):
    high = x.astype(BF16).astype(F32)
    return jnp.concatenate([high, x - high], axis=0).astype(BF16)


def dot3(rows, both, b, dims=PLAIN):
    wide = dot1(both, b[0], dims)
    return wide[:rows] + wide[rows:] - dot1(both[:rows], b[1], dims)


def three_rows(x):
    high = x.astype(BF16).astype(F32)
    rest = x - high
    mid = rest.astype(BF16).astype(F32)
    return jnp.concatenate([high, mid, rest - mid], axis=0).astype(BF16)


def shift_y(x, step):
    if step == 0:
        return x
    rolled = pltpu.roll(x, (-step) % NY, 1)
    y = lax.broadcasted_iota(jnp.int32, x.shape, 1)
    keep = (y < NY - step) if step > 0 else (y >= -step)
    return jnp.where(keep, rolled, 0.0)


def pair_y(x, step):
    if step == 0:
        return x
    return shift_y(x, step) + shift_y(x, -step)


def rows2(x):
    return x.reshape(x.shape[0] * x.shape[1], x.shape[2])


def kernel(
    spaces, slabs, deltas, slot_size,
    charge_hbm, frac_hbm, x_hbm, y_hbm, z_hbm, dest_hbm, fine_hbm, coarse_hbm, rz_hbm,
    out_ref,
    charge_in, frac_in, x_in, y_in, z_in, dest_in, rz_ref, fine_tab, coarse_tab, place, send_buf, recv_buf, res_buf, ret_buf,
    in_sem, tab_sem, send_sem, recv_sem, res_sem, ret_sem,
):
    i = lax.axis_index("space")
    l = lax.axis_index("slab")
    groups = len(deltas)
    atoms = charge_in.shape[1]
    slots = spaces * slot_size
    tiles = slots // LANES
    per_tile = LANES // slot_size

    def each(first):
        return pl.loop(first, spaces, unroll=spaces <= 16)

    def peer(k, g):
        return (lax.rem(i + k, spaces), lax.rem(l + deltas[g], slabs))

    barrier = pltpu.get_barrier_semaphore()
    for g in reversed(range(groups)):
        first = 1 if g == 0 else 0

        @each(first)
        def _(k):
            pl.semaphore_signal(barrier, inc=1, device_id=peer(k, g), device_id_type=MESH)

    arguments = (
        (charge_hbm, charge_in), (frac_hbm, frac_in), (x_hbm, x_in),
        (y_hbm, y_in), (z_hbm, z_in), (dest_hbm, dest_in),
    )
    arriving = [
        pltpu.make_async_copy(a, b, in_sem) for a, b in arguments
    ]
    for copy in arriving:
        copy.start()
    fine_copy = pltpu.make_async_copy(
        fine_hbm.at[:, pl.ds(0, LEAD)], fine_tab.at[:, pl.ds(0, LEAD)], tab_sem
    )
    fine_copy2 = pltpu.make_async_copy(
        fine_hbm.at[:, pl.ds(LEAD, TAIL)], fine_tab.at[:, pl.ds(WIDE - TAIL, TAIL)], tab_sem
    )
    coarse_copy = pltpu.make_async_copy(coarse_hbm, coarse_tab, tab_sem)
    fine_copy.start()
    fine_copy2.start()
    coarse_copy.start()
    rz_copy = pltpu.make_async_copy(rz_hbm, rz_ref, tab_sem)
    rz_copy.start()

    for edge in (0, spaces + 1):
        send_buf[edge] = jnp.zeros(send_buf.shape[1:], F32)

    for copy in arriving:
        copy.wait()
    dest = dest_in[...].astype(F32)
    payload = jnp.concatenate(
        [
            charge_in[...],
            frac_in[...],
            x_in[...].astype(F32),
            y_in[...].astype(F32),
            z_in[...].astype(F32),
            dest,
        ],
        axis=0,
    )
    chosen = (
        lax.broadcasted_iota(jnp.int32, (spaces, atoms), 0).astype(F32) == dest
    ).astype(F32)
    earlier = (
        lax.broadcasted_iota(jnp.int32, (atoms, atoms), 0)
        < lax.broadcasted_iota(jnp.int32, (atoms, atoms), 1)
    ).astype(F32).astype(BF16)
    counts = dot1(chosen.astype(BF16), earlier)
    rank = jnp.sum(chosen * counts, axis=0, keepdims=True)
    slot = dest * float(slot_size) + rank
    place[...] = (
        lax.broadcasted_iota(jnp.int32, (slots, atoms), 0).astype(F32) == slot
    ).astype(F32).astype(BF16)
    parts = dot1(three_rows(payload), place[...], TURNED)
    packed = parts[0:8] + parts[8:16] + parts[16:24]
    lane_part = lax.broadcasted_iota(jnp.int32, (8, LANES), 1) // slot_size
    row_part = lax.rem(lax.broadcasted_iota(jnp.int32, (8, LANES), 0), per_tile)
    columns = min(8, per_tile)

    def compact(value, count, out, skip=0):
        for q in range(tiles):
            tile = value[:, q * LANES : (q + 1) * LANES]
            turned = [pltpu.roll(tile, n * slot_size, 1) if n else tile for n in range(per_tile)]
            for r in range(per_tile):
                merged = jnp.zeros((8, LANES), F32)
                for c in range(columns):
                    here = (lane_part == c) & (row_part == c)
                    merged = jnp.where(here, turned[(c - r) % per_tile], merged)
                for n in range(-(-count // per_tile)):
                    rows = merged[n * columns : (n + 1) * columns]
                    out[q * per_tile + r + skip, n : n + 1] = jnp.sum(rows, axis=0, keepdims=True)

    compact(packed, 8, send_buf, 1)

    fine_tab[:, LEAD : WIDE - TAIL] = jnp.zeros(
        (fine_tab.shape[0], WIDE - TAIL - LEAD, WIDE), BF16
    )
    pl.semaphore_wait(barrier, groups * spaces - 1)

    def atom_copy(k, g):
        target = peer(k, g)
        return pltpu.make_async_remote_copy(
            src_ref=send_buf.at[pl.ds(target[0], 3)],
            dst_ref=recv_buf.at[g, i],
            send_sem=send_sem,
            recv_sem=recv_sem,
            device_id=target,
            device_id_type=MESH,
        )

    def arrived(ref, sem):
        return pltpu.make_async_copy(ref, ref, sem)

    for g in reversed(range(groups)):

        @each(1 if g == 0 else 0)
        def _(k):
            atom_copy(k, g).start()

    own_atoms = pltpu.make_async_copy(send_buf.at[pl.ds(i, 3)], recv_buf.at[0, i], recv_sem)
    own_atoms.start()

    def regroup(piece_of):
        out = []
        for q in range(tiles):
            total = jnp.zeros((8, LANES), F32)
            for r in range(per_tile):
                piece = piece_of(q * per_tile + r)
                repeated = [
                    jnp.broadcast_to(piece[n : n + 1], (columns, LANES))
                    for n in range(piece.shape[0])
                ]
                while len(repeated) * columns < 8:
                    repeated.append(jnp.zeros((columns, LANES), F32))
                spread = jnp.concatenate(repeated, axis=0)
                for c in range(columns):
                    turn = (r - c) % per_tile * slot_size
                    turned = pltpu.roll(spread, turn, 1) if turn else spread
                    total = jnp.where((lane_part == r) & (row_part == c), turned, total)
            out.append(total)
        return jnp.concatenate(out, axis=1)

    def spline(t):
        u = 1.0 - t
        t2 = t * t
        t3 = t2 * t
        w = (
            u * u * u / 6.0,
            (3.0 * t3 - 6.0 * t2 + 4.0) / 6.0,
            (-3.0 * t3 + 3.0 * t2 + 3.0 * t + 1.0) / 6.0,
            t3 / 6.0,
        )
        s = (
            -u * u / 2.0,
            (3.0 * t2 - 4.0 * t) / 2.0,
            (-3.0 * t2 + 2.0 * t + 1.0) / 2.0,
            t2 / 2.0,
        )
        return w, s

    def spread_rows(weights, row, position):
        total = jnp.zeros(position.shape, F32)
        for k in range(4):
            total = jnp.where(position == float(k), weights[k][row : row + 1], total)
        return total

    row_x = lax.broadcasted_iota(jnp.int32, (24, slots), 0).astype(F32)
    row_y = lax.broadcasted_iota(jnp.int32, (NY, slots), 0).astype(F32) + 1.0

    own_rows = ((0, CZ + 16), (WIDE - 16, WIDE))
    side_rows = ((0, 16), (CZ - 16, CZ + 16), (WIDE - 16, WIDE))

    def z_matrix(weights, base, pieces):
        def packed_rows(v):
            return jnp.broadcast_to(v, (16, slots)).astype(BF16)

        base = packed_rows(base - 1.0)
        highs = [weights[k][3:4].astype(BF16).astype(F32) for k in range(4)]
        lows = [packed_rows(highs[k] - weights[k][3:4]) for k in range(4)]
        highs = [packed_rows(v) for v in highs]
        low_row = lax.broadcasted_iota(jnp.int32, (16, slots), 0).astype(F32)
        halves = ([], [])
        done = 0
        for first, end in pieces:
            if first > done:
                for h in halves:
                    h.append(jnp.zeros((first - done, slots), BF16))
            shift = 0 if end <= 3 * WIDE // 4 else WIDE
            for row in range(first - shift, end - shift, 16):
                lag = (low_row + float(row)).astype(BF16) - base
                high = low = jnp.zeros((16, slots), BF16)
                for k in range(4):
                    here = lag == jnp.array(k, BF16)
                    high = jnp.where(here, highs[k], high)
                    low = jnp.where(here, lows[k], low)
                halves[0].append(high)
                halves[1].append(low)
            done = end
        return tuple(jnp.concatenate(h, axis=0) for h in halves)

    fine_copy.wait()
    fine_copy2.wait()
    coarse_copy.wait()
    rz_copy.wait()
    arrived(recv_buf, recv_sem).wait()

    def spread(part, first_row, rows):
        planes, zs, kept = [], [], None
        for g in range(groups):
            got = regroup(lambda j: recv_buf[g, j, part])
            w, s = spline(got)
            mx = spread_rows(w, 1, row_x - got[4:5])
            my = spread_rows(w, 2, row_y - got[5:6])
            z_off = ((lax.rem(l - deltas[g] + slabs, slabs) - l) * CZ).astype(F32)
            z_base = got[6:7] + z_off
            mz = z_matrix(w, z_base, side_rows if g else own_rows)
            if g == 0:
                kept = (w, s, got, mx, my, mz)
            cx = got[0:1] * mx
            plane = jnp.concatenate(
                [cx[x : x + 1] * my for x in range(first_row, first_row + rows)], axis=0
            )
            planes.append(two_rows(plane))
            zs.append(mz)
        plane2 = jnp.concatenate(planes, axis=1)
        z2 = [jnp.concatenate([z[h] for z in zs], axis=1) for h in range(2)]
        return dot3(rows * NY, plane2, z2, TURNED).reshape(rows, NY, WIDE), kept

    mid, own = spread(1, 0, OUT_X)
    left, _ = spread(0, OUT_X - SIDE, SIDE)
    right, _ = spread(2, 0, SIDE)

    w, s, got, mx, my, mz_split = own
    charge = got[0:1]
    dx = spread_rows(s, 1, row_x - got[4:5])
    dy = spread_rows(s, 2, row_y - got[5:6])
    dz_split = z_matrix(s, got[6:7], own_rows)

    def inside(shape, first_x, block_x, block_z):
        ax = lax.broadcasted_iota(jnp.int32, shape, 0) + (i * block_x + first_x)
        az = lax.broadcasted_iota(jnp.int32, shape, 2)
        lanes = shape[2]
        az = jnp.where(az < 3 * lanes // 4, az, az - lanes) + l * block_z
        return (ax >= 0) & (ax < spaces * block_x) & (az >= 0) & (az < slabs * block_z)

    over = SIDE - REACH + 1
    grid = jnp.concatenate(
        [
            left[: SIDE - over],
            left[SIDE - over :] + mid[:over],
            mid[over : OUT_X - over],
            mid[OUT_X - over :] + right[:over],
            right[over:],
        ],
        axis=0,
    )
    grid = jnp.where(inside(grid.shape, -REACH, CX, CZ), grid, 0.0)

    def stencil(parts, table, full):
        near, far = parts
        rows, depth = far.shape[0], table.shape[1]
        wide = dot1(near, table[:full].reshape(full * depth, table.shape[2]))
        rest = dot1(
            jnp.concatenate([far, near[:rows]], axis=1),
            table[full:].reshape(-1, table.shape[2]),
        )
        return wide[:rows] + wide[rows:] - rest

    coarse = []
    for n in range(EXT_C):
        at = 2 * n + 2
        coarse.append(
            B0 * grid[at : at + 1]
            + B1 * (grid[at - 1 : at] + grid[at + 1 : at + 2])
            + B2 * (grid[at - 2 : at - 1] + grid[at + 2 : at + 3])
        )
    coarse = jnp.concatenate(coarse, axis=0)
    coarse = B0 * coarse + B1 * pair_y(coarse, 1) + B2 * pair_y(coarse, 2)
    high, low = two(rows2(coarse))
    rz = rz_ref[...]
    coarse = (dot1(high, rz) + dot1(low, rz)).reshape(EXT_C, NY, LANES)
    coarse = jnp.where(inside(coarse.shape, -5, CX // 2, CZ // 2), coarse, 0.0)

    def stack(source, out_count, step_y, reach_y, sums):
        shifted = [pair_y(source, step_y * d) if step_y * d < NY else None for d in range(reach_y)]
        near, far = [], []
        for square in sums:
            total = None
            for d in range(5):
                for e in range(reach_y):
                    if d * d + e * e != square:
                        continue
                    v = shifted[e]
                    term = v[4 + d : 4 + d + out_count]
                    if d:
                        term = term + v[4 - d : 4 - d + out_count]
                    total = term if total is None else total + term
            total = rows2(total)
            if square < FULL_BELOW:
                near.append(two_rows(total))
            else:
                far.append(total.astype(BF16))
        return jnp.concatenate(near, axis=1), jnp.concatenate(far, axis=1)

    lifted = stencil(
        stack(coarse, OUT_C, 2, 4, COARSE_S), coarse_tab, COARSE_FULL
    ).reshape(OUT_C, NY, LANES)
    even = lax.rem(lax.broadcasted_iota(jnp.int32, lifted.shape, 1), 2) == 0
    lifted = jnp.where(inside(lifted.shape, -1, CX // 2, CZ // 2) & even, lifted, 0.0)
    lifted = B0 * lifted + B1 * pair_y(lifted, 1) + B2 * pair_y(lifted, 2)
    high, low = two(rows2(lifted))
    lifted = (dot1(high, rz, TURNED) + dot1(low, rz, TURNED)).reshape(OUT_C, NY, WIDE)
    fine_lift = []
    for m in range(-1, CX + 2):
        n = m // 2 + 1
        if m % 2:
            fine_lift.append(B1 * (lifted[n : n + 1] + lifted[n + 1 : n + 2]))
        else:
            fine_lift.append(
                B0 * lifted[n : n + 1] + B2 * (lifted[n - 1 : n] + lifted[n + 1 : n + 2])
            )
    around = grid[REACH - 5 : REACH - 5 + OUT_X + 8]
    potential = stencil(
        stack(around, OUT_X, 1, 5, FINE_S), fine_tab, FINE_FULL
    ).reshape(OUT_X, NY, WIDE)
    potential = potential + jnp.concatenate(fine_lift, axis=0)
    potential = jnp.where(inside(potential.shape, -1, CX, CZ), potential, 0.0)

    pot = two_rows(rows2(potential))
    through_w = dot3(OUT_X * NY, pot, mz_split)
    through_d = dot3(OUT_X * NY, pot, dz_split)
    along_w = along_dx = along_dz = jnp.zeros((NY, slots), F32)
    for x in range(OUT_X):
        tw = through_w[x * NY : (x + 1) * NY]
        td = through_d[x * NY : (x + 1) * NY]
        along_w = along_w + mx[x : x + 1] * tw
        along_dx = along_dx + dx[x : x + 1] * tw
        along_dz = along_dz + mx[x : x + 1] * td

    def down(v):
        return jnp.sum(v, axis=0, keepdims=True)

    results = jnp.concatenate(
        [
            0.5 * charge * down(my * along_w),
            -charge * down(my * along_dx),
            -charge * down(dy * along_w),
            -charge * down(my * along_dz),
            jnp.zeros((4, slots), F32),
        ],
        axis=0,
    )
    compact(results, 4, res_buf)

    def result_copy(k):
        target = lax.rem(i + k, spaces)
        return pltpu.make_async_remote_copy(
            src_ref=res_buf.at[target], dst_ref=ret_buf.at[i],
            send_sem=res_sem, recv_sem=ret_sem,
            device_id=(target, l), device_id_type=MESH,
        )

    @each(1)
    def _(k):
        result_copy(k).start()

    own_results = pltpu.make_async_copy(res_buf.at[i], ret_buf.at[i], ret_sem)
    own_results.start()

    for g in range(groups):
        sent = recv_buf.at[g] if g else recv_buf.at[0, pl.ds(1, spaces - 1)]
        arrived(sent, send_sem).wait()

    arrived(ret_buf, ret_sem).wait()
    back = regroup(lambda j: ret_buf[j])
    parts = dot1(three_rows(back), place[...])
    final = parts[0:8] + parts[8:16] + parts[16:24]
    out_ref[...] = final

    arrived(ret_buf.at[pl.ds(1, spaces - 1)], res_sem).wait()


def per_device(spaces, slabs, charges, fractions, cell_x, cell_y, cell_z, destination):
    atoms = charges.shape[0]
    slot_size = 2 * atoms // spaces
    slots = spaces * slot_size
    deltas = (0,) if slabs == 1 else (0, 1) if slabs == 2 else (0, 1, slabs - 1)
    groups = len(deltas)
    fine, coarse, rz = tables()
    vmem = pl.BlockSpec(memory_space=pltpu.VMEM)
    atom_rows, result_rows = (-(-n * slot_size // LANES) for n in (8, 4))
    hbm = pl.BlockSpec(memory_space=pl.ANY)
    out = pl.pallas_call(
        functools.partial(kernel, spaces, slabs, deltas, slot_size),
        out_shape=pltpu.VMEM((8, atoms), F32),
        in_specs=[hbm] * 9,
        out_specs=vmem,
        scratch_shapes=[
            pltpu.VMEM((1, atoms), F32),
            pltpu.VMEM((3, atoms), F32),
            pltpu.VMEM((1, atoms), jnp.int32),
            pltpu.VMEM((1, atoms), jnp.int32),
            pltpu.VMEM((1, atoms), jnp.int32),
            pltpu.VMEM((1, atoms), jnp.int32),
            pltpu.VMEM(rz.shape, BF16),
            pltpu.VMEM((fine.shape[0], WIDE, WIDE), BF16),
            pltpu.VMEM(coarse.shape, BF16),
            pltpu.VMEM((slots, atoms), BF16),
            pltpu.VMEM((spaces + 2, atom_rows, LANES), F32),
            pltpu.VMEM((groups, spaces, 3, atom_rows, LANES), F32),
            pltpu.VMEM((spaces, result_rows, LANES), F32),
            pltpu.VMEM((spaces, result_rows, LANES), F32),
            *[pltpu.SemaphoreType.DMA(()) for _ in range(6)],
        ],
        compiler_params=pltpu.CompilerParams(collective_id=0, has_side_effects=True),
        name="multilevel",
    )(
        charges.reshape(1, atoms),
        fractions,
        cell_x.reshape(1, atoms),
        cell_y.reshape(1, atoms),
        cell_z.reshape(1, atoms),
        destination.reshape(1, atoms),
        jnp.asarray(fine),
        jnp.asarray(coarse),
        jnp.asarray(rz),
    )
    return out[0], out[1:4]


def solution(mesh):
    both = ("space", "slab")
    return jax.shard_map(
        functools.partial(per_device, mesh.shape["space"], mesh.shape["slab"]),
        mesh=mesh,
        in_specs=(P(both), P(None, both), P(both), P(both), P(both), P(both, None)),
        out_specs=(P(both), P(None, both)),
        check_vma=False,
    )
```

```python
import functools

import jax
import jax.numpy as jnp
import numpy as np
from jax import lax
from jax.experimental import pallas as pl
from jax.experimental.pallas import tpu as pltpu
from jax.sharding import PartitionSpec as P

CX = 16
NY = 8
CZ = 128
LANES = 128
WIDE = 2 * CZ
COULOMB = 332.0636 / 2.5
B0, B1, B2 = 0.75, 0.5, 0.125
OUT_X = CX + 3
REACH = 12
SIDE = REACH + 2
EXT_X = REACH + CX + REACH + 1
OUT_C = CX // 2 + 3
EXT_C = OUT_C + 8
FINE_S = sorted({a * a + b * b for a in range(5) for b in range(5)})
COARSE_S = sorted({a * a + b * b for a in range(5) for b in range(4)})
FULL_BELOW = 13
FINE_FULL = sum(s < FULL_BELOW for s in FINE_S)
COARSE_FULL = sum(s < FULL_BELOW for s in COARSE_S)
LEAD, TAIL = CZ + 16, 16
MESH = pl.DeviceIdType.MESH
F32 = jnp.float32
BF16 = jnp.bfloat16


def np_gamma(r):
    sq = r * r
    return np.where(r < 1.0, 1.875 - 1.25 * sq + 0.375 * sq * sq, 1.0 / np.maximum(r, 1.0))


def np_stencil(squares, level):
    r = np.sqrt(squares.astype(np.float64)) * 2.0**level
    c = 2.0 * 2.0**level
    return COULOMB * (np_gamma(r / c) / c - np_gamma(r / (2 * c)) / (2 * c))


def np_cells(count):
    lane = np.arange(count)
    return np.where(lane < 3 * count // 4, lane, lane - count)


def tables():
    def banded(cells, level, sums):
        lag = cells[:, None] - cells[None, :]
        parts = [np.where(abs(lag) <= 4, np_stencil(s + lag * lag, level), 0.0) for s in sums]
        return np.stack(parts).astype(np.float32)

    def split(t, full):
        high = t.astype(BF16)
        low = (t - high.astype(np.float32)).astype(BF16)
        return np.concatenate([high[:full], -high[full:], -low[:full]], axis=0)

    fine_cells, coarse_cells = np_cells(WIDE), np_cells(LANES)
    off = abs(fine_cells[:, None] - 2 * coarse_cells[None, :])
    rz = np.where(off == 0, B0, np.where(off == 1, B1, np.where(off == 2, B2, 0.0))).astype(BF16)
    fine = split(banded(fine_cells, 0, FINE_S), FINE_FULL)
    fine = np.concatenate([fine[:, :LEAD], fine[:, WIDE - TAIL :]], axis=1)
    return fine, split(banded(coarse_cells, 1, COARSE_S), COARSE_FULL), rz


def two(x):
    high = x.astype(BF16)
    return high, (x - high.astype(F32)).astype(BF16)


PLAIN = (((1,), (0,)), ((), ()))
TURNED = (((1,), (1,)), ((), ()))


def dot1(a, b, dims=PLAIN):
    return lax.dot_general(a, b, dims, preferred_element_type=F32)


def two_rows(x):
    high = x.astype(BF16).astype(F32)
    return jnp.concatenate([high, x - high], axis=0).astype(BF16)


def dot3(rows, both, b, dims=PLAIN):
    wide = dot1(both, b[0], dims)
    return wide[:rows] + wide[rows:] - dot1(both[:rows], b[1], dims)


def three_rows(x):
    high = x.astype(BF16).astype(F32)
    rest = x - high
    mid = rest.astype(BF16).astype(F32)
    return jnp.concatenate([high, mid, rest - mid], axis=0).astype(BF16)


def shift_y(x, step):
    if step == 0:
        return x
    rolled = pltpu.roll(x, (-step) % NY, 1)
    y = lax.broadcasted_iota(jnp.int32, x.shape, 1)
    keep = (y < NY - step) if step > 0 else (y >= -step)
    return jnp.where(keep, rolled, 0.0)


def pair_y(x, step):
    if step == 0:
        return x
    return shift_y(x, step) + shift_y(x, -step)


def rows2(x):
    return x.reshape(x.shape[0] * x.shape[1], x.shape[2])


def kernel(
    spaces, slabs, deltas, slot_size,
    charge_hbm, frac_hbm, x_hbm, y_hbm, z_hbm, dest_hbm, fine_hbm, coarse_hbm, rz_hbm,
    out_ref,
    charge_in, frac_in, x_in, y_in, z_in, dest_in, rz_ref, fine_tab, coarse_tab, place, send_buf, recv_buf, res_buf, ret_buf,
    in_sem, tab_sem, send_sem, recv_sem, res_sem, ret_sem,
):
    i = lax.axis_index("space")
    l = lax.axis_index("slab")
    groups = len(deltas)
    atoms = charge_in.shape[1]
    slots = spaces * slot_size
    tiles = slots // LANES
    per_tile = LANES // slot_size

    def each(first):
        return pl.loop(first, spaces, unroll=spaces <= 16)

    def peer(k, g):
        return (lax.rem(i + k, spaces), lax.rem(l + deltas[g], slabs))

    barrier = pltpu.get_barrier_semaphore()
    @each(1)
    def _(k):
        for g in reversed(range(groups)):
            pl.semaphore_signal(barrier, inc=1, device_id=peer(k, g), device_id_type=MESH)

    for g in range(1, groups):
        pl.semaphore_signal(barrier, inc=1, device_id=peer(0, g), device_id_type=MESH)

    arguments = (
        (charge_hbm, charge_in), (frac_hbm, frac_in), (x_hbm, x_in),
        (y_hbm, y_in), (z_hbm, z_in), (dest_hbm, dest_in),
    )
    arriving = [
        pltpu.make_async_copy(a, b, in_sem) for a, b in arguments
    ]
    for copy in arriving:
        copy.start()
    fine_copy = pltpu.make_async_copy(
        fine_hbm.at[:, pl.ds(0, LEAD)], fine_tab.at[:, pl.ds(0, LEAD)], tab_sem
    )
    fine_copy2 = pltpu.make_async_copy(
        fine_hbm.at[:, pl.ds(LEAD, TAIL)], fine_tab.at[:, pl.ds(WIDE - TAIL, TAIL)], tab_sem
    )
    coarse_copy = pltpu.make_async_copy(coarse_hbm, coarse_tab, tab_sem)
    fine_copy.start()
    fine_copy2.start()
    coarse_copy.start()
    rz_copy = pltpu.make_async_copy(rz_hbm, rz_ref, tab_sem)
    rz_copy.start()

    for edge in (0, spaces + 1):
        send_buf[edge] = jnp.zeros(send_buf.shape[1:], F32)

    for copy in arriving:
        copy.wait()
    dest = dest_in[...].astype(F32)
    payload = jnp.concatenate(
        [
            charge_in[...],
            frac_in[...],
            x_in[...].astype(F32),
            y_in[...].astype(F32),
            z_in[...].astype(F32),
            dest,
        ],
        axis=0,
    )
    chosen = (
        lax.broadcasted_iota(jnp.int32, (spaces, atoms), 0).astype(F32) == dest
    ).astype(F32)
    earlier = (
        lax.broadcasted_iota(jnp.int32, (atoms, atoms), 0)
        < lax.broadcasted_iota(jnp.int32, (atoms, atoms), 1)
    ).astype(F32).astype(BF16)
    counts = dot1(chosen.astype(BF16), earlier)
    rank = jnp.sum(chosen * counts, axis=0, keepdims=True)
    slot = dest * float(slot_size) + rank
    place[...] = (
        lax.broadcasted_iota(jnp.int32, (slots, atoms), 0).astype(F32) == slot
    ).astype(F32).astype(BF16)
    parts = dot1(three_rows(payload), place[...], TURNED)
    packed = parts[0:8] + parts[8:16] + parts[16:24]
    lane_part = lax.broadcasted_iota(jnp.int32, (8, LANES), 1) // slot_size
    row_part = lax.rem(lax.broadcasted_iota(jnp.int32, (8, LANES), 0), per_tile)
    columns = min(8, per_tile)

    def compact(value, count, out, skip=0):
        for q in range(tiles):
            tile = value[:, q * LANES : (q + 1) * LANES]
            turned = [pltpu.roll(tile, n * slot_size, 1) if n else tile for n in range(per_tile)]
            for r in range(per_tile):
                merged = jnp.zeros((8, LANES), F32)
                for c in range(columns):
                    here = (lane_part == c) & (row_part == c)
                    merged = jnp.where(here, turned[(c - r) % per_tile], merged)
                for n in range(-(-count // per_tile)):
                    rows = merged[n * columns : (n + 1) * columns]
                    out[q * per_tile + r + skip, n : n + 1] = jnp.sum(rows, axis=0, keepdims=True)

    compact(packed, 8, send_buf, 1)

    fine_tab[:, LEAD : WIDE - TAIL] = jnp.zeros(
        (fine_tab.shape[0], WIDE - TAIL - LEAD, WIDE), BF16
    )
    pl.semaphore_wait(barrier, groups * spaces - 1)

    def atom_copy(k, g):
        target = peer(spaces - k, g)
        return pltpu.make_async_remote_copy(
            src_ref=send_buf.at[pl.ds(target[0], 3)],
            dst_ref=recv_buf.at[g, i],
            send_sem=send_sem,
            recv_sem=recv_sem,
            device_id=target,
            device_id_type=MESH,
        )

    def arrived(ref, sem):
        return pltpu.make_async_copy(ref, ref, sem)

    @each(1)
    def _(k):
        for g in reversed(range(groups)):
            atom_copy(k, g).start()

    for g in range(1, groups):
        atom_copy(0, g).start()

    own_atoms = pltpu.make_async_copy(send_buf.at[pl.ds(i, 3)], recv_buf.at[0, i], recv_sem)
    own_atoms.start()

    def regroup(piece_of):
        out = []
        for q in range(tiles):
            total = jnp.zeros((8, LANES), F32)
            for r in range(per_tile):
                piece = piece_of(q * per_tile + r)
                repeated = [
                    jnp.broadcast_to(piece[n : n + 1], (columns, LANES))
                    for n in range(piece.shape[0])
                ]
                while len(repeated) * columns < 8:
                    repeated.append(jnp.zeros((columns, LANES), F32))
                spread = jnp.concatenate(repeated, axis=0)
                for c in range(columns):
                    turn = (r - c) % per_tile * slot_size
                    turned = pltpu.roll(spread, turn, 1) if turn else spread
                    total = jnp.where((lane_part == r) & (row_part == c), turned, total)
            out.append(total)
        return jnp.concatenate(out, axis=1)

    def spline(t):
        u = 1.0 - t
        t2 = t * t
        t3 = t2 * t
        w = (
            u * u * u / 6.0,
            (3.0 * t3 - 6.0 * t2 + 4.0) / 6.0,
            (-3.0 * t3 + 3.0 * t2 + 3.0 * t + 1.0) / 6.0,
            t3 / 6.0,
        )
        s = (
            -u * u / 2.0,
            (3.0 * t2 - 4.0 * t) / 2.0,
            (-3.0 * t2 + 2.0 * t + 1.0) / 2.0,
            t2 / 2.0,
        )
        return w, s

    def spread_rows(weights, row, position):
        total = jnp.zeros(position.shape, F32)
        for k in range(4):
            total = jnp.where(position == float(k), weights[k][row : row + 1], total)
        return total

    row_x = lax.broadcasted_iota(jnp.int32, (24, slots), 0).astype(F32)
    row_y = lax.broadcasted_iota(jnp.int32, (NY, slots), 0).astype(F32) + 1.0

    own_rows = ((0, CZ + 16), (WIDE - 16, WIDE))
    side_rows = ((0, 16), (CZ - 16, CZ + 16), (WIDE - 16, WIDE))

    def z_matrix(weights, base, pieces):
        def packed_rows(v):
            return jnp.broadcast_to(v, (16, slots)).astype(BF16)

        base = packed_rows(base - 1.0)
        highs = [weights[k][3:4].astype(BF16).astype(F32) for k in range(4)]
        lows = [packed_rows(highs[k] - weights[k][3:4]) for k in range(4)]
        highs = [packed_rows(v) for v in highs]
        low_row = lax.broadcasted_iota(jnp.int32, (16, slots), 0).astype(F32)
        halves = ([], [])
        done = 0
        for first, end in pieces:
            if first > done:
                for h in halves:
                    h.append(jnp.zeros((first - done, slots), BF16))
            shift = 0 if end <= 3 * WIDE // 4 else WIDE
            for row in range(first - shift, end - shift, 16):
                lag = (low_row + float(row)).astype(BF16) - base
                high = low = jnp.zeros((16, slots), BF16)
                for k in range(4):
                    here = lag == jnp.array(k, BF16)
                    high = jnp.where(here, highs[k], high)
                    low = jnp.where(here, lows[k], low)
                halves[0].append(high)
                halves[1].append(low)
            done = end
        return tuple(jnp.concatenate(h, axis=0) for h in halves)

    fine_copy.wait()
    fine_copy2.wait()
    coarse_copy.wait()
    rz_copy.wait()
    arrived(recv_buf, recv_sem).wait()

    def spread(part, first_row, rows):
        planes, zs, kept = [], [], None
        for g in range(groups):
            got = regroup(lambda j: recv_buf[g, j, part])
            w, s = spline(got)
            mx = spread_rows(w, 1, row_x - got[4:5])
            my = spread_rows(w, 2, row_y - got[5:6])
            z_off = ((lax.rem(l - deltas[g] + slabs, slabs) - l) * CZ).astype(F32)
            z_base = got[6:7] + z_off
            mz = z_matrix(w, z_base, side_rows if g else own_rows)
            if g == 0:
                kept = (w, s, got, mx, my, mz)
            cx = got[0:1] * mx
            plane = jnp.concatenate(
                [cx[x : x + 1] * my for x in range(first_row, first_row + rows)], axis=0
            )
            planes.append(two_rows(plane))
            zs.append(mz)
        plane2 = jnp.concatenate(planes, axis=1)
        z2 = [jnp.concatenate([z[h] for z in zs], axis=1) for h in range(2)]
        return dot3(rows * NY, plane2, z2, TURNED).reshape(rows, NY, WIDE), kept

    mid, own = spread(1, 0, OUT_X)
    left, _ = spread(0, OUT_X - SIDE, SIDE)
    right, _ = spread(2, 0, SIDE)

    w, s, got, mx, my, mz_split = own
    charge = got[0:1]
    dx = spread_rows(s, 1, row_x - got[4:5])
    dy = spread_rows(s, 2, row_y - got[5:6])
    dz_split = z_matrix(s, got[6:7], own_rows)

    def inside(shape, first_x, block_x, block_z):
        ax = lax.broadcasted_iota(jnp.int32, shape, 0) + (i * block_x + first_x)
        az = lax.broadcasted_iota(jnp.int32, shape, 2)
        lanes = shape[2]
        az = jnp.where(az < 3 * lanes // 4, az, az - lanes) + l * block_z
        return (ax >= 0) & (ax < spaces * block_x) & (az >= 0) & (az < slabs * block_z)

    over = SIDE - REACH + 1
    grid = jnp.concatenate(
        [
            left[: SIDE - over],
            left[SIDE - over :] + mid[:over],
            mid[over : OUT_X - over],
            mid[OUT_X - over :] + right[:over],
            right[over:],
        ],
        axis=0,
    )
    grid = jnp.where(inside(grid.shape, -REACH, CX, CZ), grid, 0.0)

    def stencil(parts, table, full):
        near, far = parts
        rows, depth = far.shape[0], table.shape[1]
        wide = dot1(near, table[:full].reshape(full * depth, table.shape[2]))
        rest = dot1(
            jnp.concatenate([far, near[:rows]], axis=1),
            table[full:].reshape(-1, table.shape[2]),
        )
        return wide[:rows] + wide[rows:] - rest

    coarse = []
    for n in range(EXT_C):
        at = 2 * n + 2
        coarse.append(
            B0 * grid[at : at + 1]
            + B1 * (grid[at - 1 : at] + grid[at + 1 : at + 2])
            + B2 * (grid[at - 2 : at - 1] + grid[at + 2 : at + 3])
        )
    coarse = jnp.concatenate(coarse, axis=0)
    coarse = B0 * coarse + B1 * pair_y(coarse, 1) + B2 * pair_y(coarse, 2)
    high, low = two(rows2(coarse))
    rz = rz_ref[...]
    coarse = (dot1(high, rz) + dot1(low, rz)).reshape(EXT_C, NY, LANES)
    coarse = jnp.where(inside(coarse.shape, -5, CX // 2, CZ // 2), coarse, 0.0)

    def stack(source, out_count, step_y, reach_y, sums):
        shifted = [pair_y(source, step_y * d) if step_y * d < NY else None for d in range(reach_y)]
        near, far = [], []
        for square in sums:
            total = None
            for d in range(5):
                for e in range(reach_y):
                    if d * d + e * e != square:
                        continue
                    v = shifted[e]
                    term = v[4 + d : 4 + d + out_count]
                    if d:
                        term = term + v[4 - d : 4 - d + out_count]
                    total = term if total is None else total + term
            total = rows2(total)
            if square < FULL_BELOW:
                near.append(two_rows(total))
            else:
                far.append(total.astype(BF16))
        return jnp.concatenate(near, axis=1), jnp.concatenate(far, axis=1)

    lifted = stencil(
        stack(coarse, OUT_C, 2, 4, COARSE_S), coarse_tab, COARSE_FULL
    ).reshape(OUT_C, NY, LANES)
    even = lax.rem(lax.broadcasted_iota(jnp.int32, lifted.shape, 1), 2) == 0
    lifted = jnp.where(inside(lifted.shape, -1, CX // 2, CZ // 2) & even, lifted, 0.0)
    lifted = B0 * lifted + B1 * pair_y(lifted, 1) + B2 * pair_y(lifted, 2)
    high, low = two(rows2(lifted))
    lifted = (dot1(high, rz, TURNED) + dot1(low, rz, TURNED)).reshape(OUT_C, NY, WIDE)
    fine_lift = []
    for m in range(-1, CX + 2):
        n = m // 2 + 1
        if m % 2:
            fine_lift.append(B1 * (lifted[n : n + 1] + lifted[n + 1 : n + 2]))
        else:
            fine_lift.append(
                B0 * lifted[n : n + 1] + B2 * (lifted[n - 1 : n] + lifted[n + 1 : n + 2])
            )
    around = grid[REACH - 5 : REACH - 5 + OUT_X + 8]
    potential = stencil(
        stack(around, OUT_X, 1, 5, FINE_S), fine_tab, FINE_FULL
    ).reshape(OUT_X, NY, WIDE)
    potential = potential + jnp.concatenate(fine_lift, axis=0)
    potential = jnp.where(inside(potential.shape, -1, CX, CZ), potential, 0.0)

    pot = two_rows(rows2(potential))
    through_w = dot3(OUT_X * NY, pot, mz_split)
    through_d = dot3(OUT_X * NY, pot, dz_split)
    along_w = along_dx = along_dz = jnp.zeros((NY, slots), F32)
    for x in range(OUT_X):
        tw = through_w[x * NY : (x + 1) * NY]
        td = through_d[x * NY : (x + 1) * NY]
        along_w = along_w + mx[x : x + 1] * tw
        along_dx = along_dx + dx[x : x + 1] * tw
        along_dz = along_dz + mx[x : x + 1] * td

    def down(v):
        return jnp.sum(v, axis=0, keepdims=True)

    results = jnp.concatenate(
        [
            0.5 * charge * down(my * along_w),
            -charge * down(my * along_dx),
            -charge * down(dy * along_w),
            -charge * down(my * along_dz),
            jnp.zeros((4, slots), F32),
        ],
        axis=0,
    )
    compact(results, 4, res_buf)

    def result_copy(k):
        target = lax.rem(i + k, spaces)
        return pltpu.make_async_remote_copy(
            src_ref=res_buf.at[target], dst_ref=ret_buf.at[i],
            send_sem=res_sem, recv_sem=ret_sem,
            device_id=(target, l), device_id_type=MESH,
        )

    @each(1)
    def _(k):
        result_copy(k).start()

    own_results = pltpu.make_async_copy(res_buf.at[i], ret_buf.at[i], ret_sem)
    own_results.start()

    for g in range(groups):
        sent = recv_buf.at[g] if g else recv_buf.at[0, pl.ds(1, spaces - 1)]
        arrived(sent, send_sem).wait()

    arrived(ret_buf, ret_sem).wait()
    back = regroup(lambda j: ret_buf[j])
    parts = dot1(three_rows(back), place[...])
    final = parts[0:8] + parts[8:16] + parts[16:24]
    out_ref[...] = final

    arrived(ret_buf.at[pl.ds(1, spaces - 1)], res_sem).wait()


def per_device(spaces, slabs, charges, fractions, cell_x, cell_y, cell_z, destination):
    atoms = charges.shape[0]
    slot_size = 2 * atoms // spaces
    slots = spaces * slot_size
    deltas = (0,) if slabs == 1 else (0, 1) if slabs == 2 else (0, 1, slabs - 1)
    groups = len(deltas)
    fine, coarse, rz = tables()
    vmem = pl.BlockSpec(memory_space=pltpu.VMEM)
    atom_rows, result_rows = (-(-n * slot_size // LANES) for n in (8, 4))
    hbm = pl.BlockSpec(memory_space=pl.ANY)
    out = pl.pallas_call(
        functools.partial(kernel, spaces, slabs, deltas, slot_size),
        out_shape=pltpu.VMEM((8, atoms), F32),
        in_specs=[hbm] * 9,
        out_specs=vmem,
        scratch_shapes=[
            pltpu.VMEM((1, atoms), F32),
            pltpu.VMEM((3, atoms), F32),
            pltpu.VMEM((1, atoms), jnp.int32),
            pltpu.VMEM((1, atoms), jnp.int32),
            pltpu.VMEM((1, atoms), jnp.int32),
            pltpu.VMEM((1, atoms), jnp.int32),
            pltpu.VMEM(rz.shape, BF16),
            pltpu.VMEM((fine.shape[0], WIDE, WIDE), BF16),
            pltpu.VMEM(coarse.shape, BF16),
            pltpu.VMEM((slots, atoms), BF16),
            pltpu.VMEM((spaces + 2, atom_rows, LANES), F32),
            pltpu.VMEM((groups, spaces, 3, atom_rows, LANES), F32),
            pltpu.VMEM((spaces, result_rows, LANES), F32),
            pltpu.VMEM((spaces, result_rows, LANES), F32),
            *[pltpu.SemaphoreType.DMA(()) for _ in range(6)],
        ],
        compiler_params=pltpu.CompilerParams(collective_id=0, has_side_effects=True),
        name="multilevel",
    )(
        charges.reshape(1, atoms),
        fractions,
        cell_x.reshape(1, atoms),
        cell_y.reshape(1, atoms),
        cell_z.reshape(1, atoms),
        destination.reshape(1, atoms),
        jnp.asarray(fine),
        jnp.asarray(coarse),
        jnp.asarray(rz),
    )
    return out[0], out[1:4]


def solution(mesh):
    both = ("space", "slab")
    return jax.shard_map(
        functools.partial(per_device, mesh.shape["space"], mesh.shape["slab"]),
        mesh=mesh,
        in_specs=(P(both), P(None, both), P(both), P(both), P(both), P(both, None)),
        out_specs=(P(both), P(None, both)),
        check_vma=False,
    )
```
